512 devices in a mesh: gy: 128 (over y, x, z_lo, core), gz: 4 (over z_hi).
Axes of the slice: x: 4, y: 4, z: 16 (z_hi: 4, z_lo: 4; z = z_hi * 4 + z_lo), core: 2. Of those that a mesh axis runs over, the one named last changes fastest.
Arguments:
- volume: float32 [160, 128, 4096], P('gz', 'gy'), may hold values from -6 to 6
- x_offsets: int32 [160], replicated, may hold values from -64 to 64, as said below
- x_fracs: float32 [160], replicated, may hold values from 0 to 1
- z_offsets: int32 [128], P('gy'), may hold values from -4 to 4, as said below
- z_fracs: float32 [128], P('gy'), may hold values from 0 to 1
- y_offsets: int32 [4096], P('gy'), may hold values from -32 to 32, as said below
- y_fracs: float32 [4096], P('gy'), may hold values from 0 to 1
- slopes: int32 [8], replicated, may hold values from -4 to 4, as said below
Outputs:
- rotated: float32 [160, 128, 4096], P('gz', 'gy')
- projections: float32 [8, 4096, 128], P('gz', 'gy')
The draws below stay inside these ranges and needn't reach their ends.
Inputs may be any that keep to these rules, and one draw needn't show every extreme that they name: `x_offsets`: each value between -64 and 64, both ends taken by some plane. `z_offsets`: each value between -4 and 4, both ends taken by some row. `y_offsets`: each value between -32 and 32, both ends taken by some column. `slopes`: each value between -4 and 4, both ends taken by some tilt.
All inputs are finite; a program needn't handle non-finite values.
Results may differ from the reference program's by a relative error of at most 0.0003.
Values sent between devices are 32-bit elements; how exact they have to be, the bound alone decides.
A program may use at most 64 MiB of HBM per device.

```python
import jax
import jax.numpy as jnp
from jax import lax

X = 4096
TAPS = 64
OFFX = 64
OFFZ = 4
TILTS = 8
SLOPE = 4
NY = 128
NZ = 160
OFFY = 32


def bounded_offsets(key, count_total, reach):
    values = jax.random.randint(key, (count_total,), -reach, reach + 1)
    places = jax.random.permutation(jax.random.fold_in(key, 7), count_total)
    values = values.at[places[0]].set(-reach)
    values = values.at[places[1]].set(reach)
    return values.astype(jnp.int32)


def draw_x_offsets(key, part):
    return bounded_offsets(jax.random.fold_in(key, 11), NZ, OFFX)


def draw_z_offsets(key, part):
    return bounded_offsets(jax.random.fold_in(key, 13), NY, OFFZ)


def draw_y_offsets(key, part):
    return bounded_offsets(jax.random.fold_in(key, 17), X, OFFY)


def draw_slopes(key, part):
    return bounded_offsets(jax.random.fold_in(key, 19), TILTS, SLOPE)


def level_of(own_key, extent, shards, smallest, top_value):
    level, own = 1.0, jax.random.fold_in(own_key, 6)
    for position, blocks in shards:
        draws = jnp.exp(jax.random.uniform(jax.random.fold_in(own, position), (blocks,), jnp.float32, smallest / len(shards), top_value / len(shards)))
        level = level * jnp.repeat(draws, extent[position] // blocks).reshape([-1 if axis == position else 1 for axis in range(len(extent))])
    return level


def normal_values(key, dims, scale, most, pieces=(), held_as=jnp.bfloat16):
    entries = scale * jax.random.normal(key, dims, jnp.float32)
    if pieces:
        entries = entries * level_of(key, dims, pieces, -0.22, 0.18)
    return jnp.clip(entries, -most, most).astype(held_as)


def setup_inputs(seed: int = 0) -> dict:
    arg_keys = jax.random.split(jax.random.key(seed), 9)
    return {
        "volume": normal_values(arg_keys[0], (NZ, NY, X), 1.0, 6.0, ((0, 4), (1, 128)), jnp.float32),
        "x_offsets": draw_x_offsets(jax.random.fold_in(arg_keys[8], 71), 0),
        "x_fracs": jnp.clip(jax.random.uniform(arg_keys[2], (NZ,), jnp.float32, 0.0, 1.0), 0.0, 1.0),
        "z_offsets": draw_z_offsets(jax.random.fold_in(arg_keys[8], 71), 0),
        "z_fracs": jnp.clip(1.0 * jax.random.uniform(arg_keys[4], (NY,), jnp.float32) ** level_of(arg_keys[4], (NY,), ((0, 128),), -0.2, 0.2), 0.0, 1.0),
        "y_offsets": draw_y_offsets(jax.random.fold_in(arg_keys[8], 71), 0),
        "y_fracs": jnp.clip(1.0 * jax.random.uniform(arg_keys[6], (X,), jnp.float32) ** level_of(arg_keys[6], (X,), ((0, 128),), -0.2, 0.2), 0.0, 1.0),
        "slopes": draw_slopes(jax.random.fold_in(arg_keys[8], 71), 0),
    }


def tap_weight(offset, fraction):
    moved = offset.astype(jnp.float32) - fraction
    inside = (offset >= 1 - TAPS // 2) & (offset <= TAPS // 2)
    value = jnp.sinc(moved) * (0.5 + 0.5 * jnp.cos(jnp.pi * moved / (TAPS // 2 + 1)))
    return jnp.where(inside, value, jnp.zeros_like(value))


def shift_lines(lines, shifts, fractions, margin):
    length = lines.shape[1]
    padded = jnp.pad(lines, ((0, 0), (margin, margin)))
    starts = (margin + shifts - (TAPS // 2 - 1)).astype(jnp.int32)
    spans = jax.vmap(lambda one_row, first_index: lax.dynamic_slice_in_dim(one_row, first_index, length + TAPS - 1))(padded, starts)
    offsets = (jnp.arange(TAPS) - (TAPS // 2 - 1)).astype(jnp.int32)
    weights = tap_weight(offsets[None, :], fractions[:, None])
    result = jnp.zeros(lines.shape, jnp.float32)
    for tap_index in range(TAPS):
        result = result + weights[:, tap_index:tap_index + 1] * spans[:, tap_index:tap_index + length]
    return result


def reference(volume, x_offsets, x_fracs, z_offsets, z_fracs, y_offsets, y_fracs, slopes):
    def shear_plane(items):
        plane, shift_value, frac_value = items
        return shift_lines(plane, jnp.full((NY,), shift_value), jnp.full((NY,), frac_value), OFFX + TAPS)

    sheared_x = lax.map(shear_plane, (volume, x_offsets, x_fracs))

    def shear_row(row_index):
        slab = lax.dynamic_index_in_dim(sheared_x, row_index, 1, keepdims=False)
        shift_value = lax.dynamic_index_in_dim(z_offsets, row_index, 0, keepdims=False)
        frac_value = lax.dynamic_index_in_dim(z_fracs, row_index, 0, keepdims=False)
        moved = shift_lines(slab.T, jnp.full((X,), shift_value), jnp.full((X,), frac_value), OFFZ + TAPS)
        return moved.T

    sheared_z = lax.map(shear_row, jnp.arange(NY, dtype=jnp.int32))
    span_pad = NY // 4

    def step_plane(totals, plane_index):
        plane = lax.dynamic_index_in_dim(sheared_z, plane_index, 1, keepdims=False)
        turned = shift_lines(plane.T, y_offsets, y_fracs, OFFY + TAPS)
        lifts = (slopes * (2 * plane_index - NZ) * NY) // (16 * NZ)
        padded = jnp.pad(turned, ((0, 0), (span_pad, span_pad)))
        moved = jax.vmap(lambda lift_one: lax.dynamic_slice_in_dim(padded, (span_pad + lift_one).astype(jnp.int32), NY, 1))(lifts)
        return totals + moved, turned.T

    start_totals = jnp.zeros((TILTS, X, NY), jnp.float32)
    totals, rotated = lax.scan(step_plane, start_totals, jnp.arange(NZ, dtype=jnp.int32))
    projections = totals * (NZ ** -0.5)
    return rotated, projections
```

```python
import functools

import jax
import jax.numpy as jnp
from jax import lax
from jax.experimental import pallas as pl
from jax.experimental.pallas import tpu as pltpu
from jax.sharding import PartitionSpec as P

TAPS = 64
ROWS = 32
PLANES = 40
DEPTH = 160
PLACES = 16
TILTS = 8
SLOPE = 4
F32 = jnp.float32
BF16 = jnp.bfloat16
VMEM_BYTES = 48 * 1024 * 1024


def tap_weight(offset, fraction):
    moved = offset.astype(F32) - fraction
    inside = (offset >= 1 - TAPS // 2) & (offset <= TAPS // 2)
    angle = jnp.pi * moved
    centre = moved == 0.0
    ratio = jnp.sin(angle) / jnp.where(centre, 1.0, angle)
    sinc = jnp.where(centre, 1.0, ratio)
    value = sinc * (0.5 + 0.5 * jnp.cos(jnp.pi * moved / (TAPS // 2 + 1)))
    return jnp.where(inside, value, 0.0)


def halves(value):
    high = value.astype(BF16)
    return high, (value - high.astype(F32)).astype(BF16)


def product(left, right):
    left_high, left_low = left
    right_high, right_low = right
    dot = functools.partial(jnp.dot, preferred_element_type=F32)
    return dot(left_high, right_high) + (dot(left_low, right_high) + dot(left_high, right_low))


def iota(shape, axis):
    return lax.broadcasted_iota(jnp.int32, shape, axis)


def band(row, rows):
    wide = jnp.broadcast_to(row, (rows, row.shape[1]))
    return pltpu.roll(wide, 0, 1, stride=1, stride_axis=0)


def shear_x(offs, fracs, y_offs, y_fracs, z_off, z_frac, planes, out, params, taps):
    first = lax.axis_index("gz") * PLANES
    sub = iota((8, 128), 0)
    for block in range(PLANES // 8):
        off = jnp.zeros((8, 128), jnp.int32)
        frac = jnp.zeros((8, 128), F32)
        for s in range(8):
            off = jnp.where(sub == s, offs[first + 8 * block + s], off)
            frac = jnp.where(sub == s, fracs[first + 8 * block + s], frac)
        for part in range(2):
            lane = iota((8, 128), 1) + 128 * part
            weights = tap_weight(128 - lane - off, frac)
            taps[8 * block : 8 * block + 8, 128 * part : 128 * part + 128] = weights
        taps[8 * block : 8 * block + 8, 256:384] = jnp.zeros((8, 128), F32)
    row = iota((ROWS, 128), 0)

    def plane(z, carry):
        matrix = band(taps[pl.ds(z, 1), :], 128)
        total = product(halves(planes[z]), halves(matrix))
        after = jnp.where(row < ROWS - 1, pltpu.roll(total[:, :128], ROWS - 1, 0), 0.0)
        before = jnp.where(row > 0, pltpu.roll(total[:, 256:], 1, 0), 0.0)
        out[pl.ds(z, ROWS, stride=PLANES), :] = total[:, 128:256] + (after + before)
        return carry

    lax.fori_loop(0, PLANES, plane, 0, unroll=4)
    params[...] = jnp.zeros((8, 128), F32)
    params[0:1, 0:32] = y_offs[...].astype(F32)
    params[1:2, 0:32] = y_fracs[...]
    params[2:3, :] = jnp.full((1, 128), z_off[0], jnp.int32).astype(F32)
    params[3:4, :] = jnp.full((1, 128), z_frac[0], F32)


def shear_z(lines, params, out, taps, mixed):
    lane = iota((8, 256), 1)
    target = jnp.where(lane < DEPTH, lane, lane - 256)
    off = params[:, 2, :][:, 0:1].astype(jnp.int32)
    frac = params[:, 3, :][:, 0:1]
    taps[...] = tap_weight(target - off, frac)

    for q in range(8):
        matrix = band(taps[q : q + 1, :], DEPTH)[:, :DEPTH]
        value = product(halves(matrix), halves(lines[q]))
        mixed[pl.ds(q, DEPTH, stride=8), :] = value
    for block in range(10):
        turned = mixed[128 * block : 128 * block + 128, :].T
        out[:, block] = turned.reshape(PLACES, 8, 128)


def exchange(values):
    group = iota((8, 128), 1) // 8
    values = list(values)
    for step in (1, 2, 4, 8):
        keep = (group // step) % 2 == 0
        for low in range(16):
            if low & step == 0:
                a, b = values[low], values[low | step]
                values[low] = jnp.where(keep, a, pltpu.roll(b, 8 * step, 1))
                values[low | step] = jnp.where(keep, pltpu.roll(a, 128 - 8 * step, 1), b)
    return values


def shear_y(slopes, blocks, params, out, projections, taps, before, after, table):
    def unpack(q, carry):
        values = exchange([blocks[p, q] for p in range(16)])
        for z in range(16):
            before[pl.ds(pl.multiple_of(128 * q + 8 * z, 8), 8), :] = values[z]
        return carry

    lax.fori_loop(0, 10, unpack, 0)
    start = 8 * (lax.axis_index("gy") // 8 % 4)
    pick = iota((8, 128), 1) == start + iota((8, 128), 0)
    off = jnp.sum(jnp.where(pick, params[0:1, :], 0.0), axis=1, keepdims=True)
    frac = jnp.sum(jnp.where(pick, params[1:2, :], 0.0), axis=1, keepdims=True)
    lane = iota((8, 256), 1)
    target = jnp.where(lane < 128, lane, lane - 256)
    taps[...] = tap_weight(-target - off.astype(jnp.int32), frac)

    for x in range(8):
        matrix = band(taps[x : x + 1, :], 128)[:, :128]
        value = product(halves(before[pl.ds(x, DEPTH, stride=8), :]), halves(matrix))
        after[pl.ds(x, DEPTH, stride=8), :] = value

    lane = iota((8, 128), 1)
    zero = jnp.zeros((8, 128), F32)
    count = 2 * SLOPE + 1
    sums, totals = [zero] * count, [zero] * count
    for z in range(DEPTH):
        value = after[8 * z : 8 * z + 8, :]
        for i in range(count):
            lift = (i - SLOPE) * (2 * z - DEPTH) * 128 // (16 * DEPTH)
            following = (i - SLOPE) * (2 * z + 2 - DEPTH) * 128 // (16 * DEPTH)
            sums[i] = sums[i] + value
            if z == DEPTH - 1 or lift != following:
                moved = sums[i]
                if lift > 0:
                    moved = jnp.where(lane < 128 - lift, pltpu.roll(moved, 128 - lift, 1), 0.0)
                elif lift < 0:
                    moved = jnp.where(lane >= -lift, pltpu.roll(moved, -lift, 1), 0.0)
                totals[i] = totals[i] + moved
                sums[i] = zero
    for i in range(count):
        table[i] = totals[i] * DEPTH ** (-0.5)
    for t in range(TILTS):
        projections[t] = table[slopes[t] + SLOPE]

    def pack(q, carry):
        rows = [after[pl.ds(pl.multiple_of(128 * q + 8 * z, 8), 8), :] for z in range(16)]
        values = exchange(rows)
        for p in range(16):
            out[p, q] = values[p]
        return carry

    lax.fori_loop(0, 10, pack, 0)


def turn_back(blocks, out):
    for block in range(10):
        turned = blocks[:, block].reshape(128, 128).T
        for z in range(16):
            out[pl.ds(16 * block + z, 8, stride=DEPTH), :] = turned[8 * z : 8 * z + 8, :]


def restore(lines, out):
    for z in range(PLANES):
        out[z] = lines[pl.ds(z, ROWS, stride=PLANES), :]


def compute(body, outs, scratch, operands, spaces, **cost):
    return pl.pallas_call(
        body,
        out_shape=outs,
        in_specs=[pl.BlockSpec(memory_space=space) for space in spaces],
        scratch_shapes=scratch,
        compiler_params=pltpu.CompilerParams(vmem_limit_bytes=VMEM_BYTES),
    )(*operands)


def position():
    g, j = lax.axis_index("gz"), lax.axis_index("gy")
    return g, j, j // 8, j % 8, g * 8 + j % 8


def copy_to(src, dst, send, recv, g, j):
    return pltpu.make_async_remote_copy(
        src_ref=src,
        dst_ref=dst,
        send_sem=send,
        recv_sem=recv,
        device_id={"gz": g, "gy": j},
        device_id_type=pl.DeviceIdType.MESH,
    )


def signal(g, j):
    pl.semaphore_signal(
        pltpu.get_barrier_semaphore(),
        inc=1,
        device_id={"gz": g, "gy": j},
        device_id_type=pl.DeviceIdType.MESH,
    )


def send_z(lines, params, out, z_params, y_params, send, recv, z_send, z_recv, y_sem, local):
    g, j, p, q, w = position()
    to_g, to_j = j // 32, (4 * (j % 4) + g) * 8 + (j // 4) % 8
    from_g, from_j = p % 4, 4 * w + p // 4
    away = jnp.logical_or(to_g != g, to_j != j)

    def greet(d, carry):
        t = (w + d) % ROWS
        signal(t // 8, 8 * p + t % 8)
        return carry

    lax.fori_loop(1, ROWS, greet, 0)
    barrier = pltpu.get_barrier_semaphore()

    @pl.when(away)
    def _():
        signal(from_g, from_j)

    pl.semaphore_wait(barrier, ROWS - 1 + away.astype(jnp.int32))

    def big(d):
        t = (w + d) % ROWS
        return copy_to(lines.at[t], out.at[q, g], send.at[d], recv.at[w], t // 8, 8 * p + t % 8)

    def landed(d):
        s = (w + ROWS - d) % ROWS
        return copy_to(lines.at[s], out.at[s % 8, s // 8], send.at[d], recv.at[s], s // 8, 8 * p + s % 8)

    def small(d):
        t = (q + d) % 8
        return copy_to(params, z_params.at[q], z_send.at[d], z_recv.at[q], g, 8 * p + t)

    def small_landed(d):
        s = (q + 8 - d) % 8
        return copy_to(params, z_params.at[s], z_send.at[d], z_recv.at[s], g, 8 * p + s)

    def loop(start, stop, act):
        def body(d, carry):
            act(d)
            return carry

        lax.fori_loop(start, stop, body, 0)

    far = copy_to(params, y_params, y_sem.at[0], y_sem.at[1], to_g, to_j)
    own_line = pltpu.make_async_copy(lines.at[w], out.at[q, g], local.at[0])
    own_z = pltpu.make_async_copy(params, z_params.at[q], local.at[1])
    own_y = pltpu.make_async_copy(params, y_params, local.at[2])

    @pl.when(away)
    def _():
        far.start()

    @pl.when(jnp.logical_not(away))
    def _():
        own_y.start()

    loop(1, 8, lambda d: small(d).start())
    loop(1, ROWS, lambda d: big(d).start())
    own_line.start()
    own_z.start()
    own_line.wait()
    own_z.wait()

    @pl.when(away)
    def _():
        far.wait_send()
        copy_to(params, y_params, y_sem.at[0], y_sem.at[1], from_g, from_j).wait_recv()

    @pl.when(jnp.logical_not(away))
    def _():
        own_y.wait()

    loop(1, 8, lambda d: small(d).wait_send())
    loop(1, 8, lambda d: small_landed(d).wait_recv())
    loop(1, ROWS, lambda d: big(d).wait_send())
    loop(1, ROWS, lambda d: landed(d).wait_recv())


def send_xy(blocks, out, send, recv, local):
    g, j, p, q, w = position()

    def greet(d, carry):
        signal(g, 8 * ((p + d) % PLACES) + q)
        return carry

    lax.fori_loop(1, PLACES, greet, 0)
    pl.semaphore_wait(pltpu.get_barrier_semaphore(), PLACES - 1)
    move_xy(blocks, out, send, recv, local)


def move_xy(blocks, out, send, recv, local):
    g, j, p, q, w = position()

    def big(d):
        t = (p + d) % PLACES
        return copy_to(blocks.at[t], out.at[p], send.at[d], recv.at[p], g, 8 * t + q)

    def landed(d):
        s = (p + PLACES - d) % PLACES
        return copy_to(blocks.at[s], out.at[s], send.at[d], recv.at[s], g, 8 * s + q)

    def loop(act):
        def body(d, carry):
            act(d)
            return carry

        lax.fori_loop(1, PLACES, body, 0)

    own = pltpu.make_async_copy(blocks.at[p], out.at[p], local.at[0])
    loop(lambda d: big(d).start())
    own.start()
    own.wait()
    loop(lambda d: big(d).wait_send())
    loop(lambda d: landed(d).wait_recv())


def send_back_xy(blocks, terms, out, projections, send, recv, local, t_send, t_recv):
    g, j, p, q, w = position()
    to_j = 4 * w + p // 4
    from_g = j // 32

    def from_j(b):
        return 8 * (4 * (j % 4) + b) + (j // 4) % 8

    def greet(d, carry):
        signal(g, 8 * ((p + d) % PLACES) + q)
        return carry

    lax.fori_loop(1, PLACES, greet, 0)
    for b in range(4):

        @pl.when(jnp.logical_or(from_g != g, from_j(b) != j))
        def _():
            signal(from_g, from_j(b))

    greeted = PLACES + 3 - (to_j == j).astype(jnp.int32)
    pl.semaphore_wait(pltpu.get_barrier_semaphore(), greeted)

    for b in range(4):
        own = pltpu.make_async_copy(terms.at[pl.ds(2 * b, 2)], projections.at[:, p % 4], local.at[1])
        copy = copy_to(
            terms.at[pl.ds(2 * b, 2)], projections.at[:, p % 4], t_send.at[b], t_recv.at[p % 4], b, to_j
        )

        @pl.when(jnp.logical_or(g != b, to_j != j))
        def _():
            copy.start()

        @pl.when(jnp.logical_not(jnp.logical_or(g != b, to_j != j)))
        def _():
            own.start()
            own.wait()

    move_xy(blocks, out, send, recv, local)
    for b in range(4):
        sent = copy_to(
            terms.at[pl.ds(2 * b, 2)], projections.at[:, p % 4], t_send.at[b], t_recv.at[p % 4], b, to_j
        )
        came = copy_to(
            terms.at[pl.ds(2 * b, 2)], projections.at[:, b], t_send.at[b], t_recv.at[b], from_g, from_j(b)
        )

        @pl.when(jnp.logical_or(g != b, to_j != j))
        def _():
            sent.wait_send()

        @pl.when(jnp.logical_or(from_g != g, from_j(b) != j))
        def _():
            came.wait_recv()


def send_back_z(lines, out, send, recv, local):
    g, j, p, q, w = position()

    def greet(d, carry):
        t = (w + d) % ROWS
        signal(t // 8, 8 * p + t % 8)
        return carry

    lax.fori_loop(1, ROWS, greet, 0)
    pl.semaphore_wait(pltpu.get_barrier_semaphore(), ROWS - 1)

    def big(d):
        t = (w + d) % ROWS
        return copy_to(lines.at[t % 8, t // 8], out.at[w], send.at[d], recv.at[w], t // 8, 8 * p + t % 8)

    def landed(d):
        s = (w + ROWS - d) % ROWS
        return copy_to(lines.at[s % 8, s // 8], out.at[s], send.at[d], recv.at[s], s // 8, 8 * p + s % 8)

    def loop(act):
        def body(d, carry):
            act(d)
            return carry

        lax.fori_loop(1, ROWS, body, 0)

    own = pltpu.make_async_copy(lines.at[q, g], out.at[w], local.at[0])
    loop(lambda d: big(d).start())
    own.start()
    own.wait()
    loop(lambda d: big(d).wait_send())
    loop(lambda d: landed(d).wait_recv())


def communicate(body, number, outs, semaphores, operands):
    return pl.pallas_call(
        body,
        out_shape=outs,
        in_specs=[pl.BlockSpec(memory_space=pl.ANY)] * len(operands),
        out_specs=jax.tree.map(lambda _: pl.BlockSpec(memory_space=pl.ANY), outs),
        scratch_shapes=[pltpu.SemaphoreType.DMA((n,)) for n in semaphores],
        compiler_params=pltpu.CompilerParams(collective_id=number, has_side_effects=True),
    )(*operands)


def local(volume, x_offsets, x_fracs, z_offsets, z_fracs, y_offsets, y_fracs, slopes):
    array = lambda *shape: jax.ShapeDtypeStruct(shape, F32)
    vmem, smem = pltpu.VMEM, pltpu.SMEM
    lines, params = compute(
        shear_x,
        (array(ROWS * PLANES, 128), array(8, 128)),
        [vmem((PLANES, 384), F32)],
        (
            x_offsets,
            x_fracs,
            y_offsets.reshape(1, 32),
            y_fracs.reshape(1, 32),
            z_offsets,
            z_fracs,
            volume.reshape(PLANES, ROWS, 128),
        ),
        (smem, smem, vmem, vmem, smem, smem, vmem),
    )
    gathered, z_params, y_params = communicate(
        send_z,
        0,
        (array(8, 4, PLANES, 128), array(8, 8, 128), array(8, 128)),
        (ROWS, ROWS, 8, 8, 2, 3),
        (lines.reshape(ROWS, PLANES, 128), params),
    )
    blocks = compute(
        shear_z,
        array(PLACES, 10, 8, 128),
        [vmem((8, 256), F32), vmem((8 * DEPTH, 128), F32)],
        (gathered.reshape(8, DEPTH, 128), z_params),
        (vmem, vmem),
    )
    columns = communicate(send_xy, 1, array(PLACES, 10, 8, 128), (PLACES, PLACES, 1), (blocks,))
    turned, terms = compute(
        shear_y,
        (array(PLACES, 10, 8, 128), array(TILTS, 8, 128)),
        [
            vmem((8, 256), F32),
            vmem((8 * DEPTH, 128), F32),
            vmem((8 * DEPTH, 128), F32),
            vmem((2 * SLOPE + 1, 8, 128), F32),
        ],
        (slopes, columns, y_params),
        (smem, vmem, vmem),
    )
    back, projections = communicate(
        send_back_xy,
        2,
        (array(PLACES, 10, 8, 128), array(2, 4, 8, 128)),
        (PLACES, PLACES, 2, 4, 4),
        (turned, terms),
    )
    rows = compute(turn_back, array(8 * DEPTH, 128), [], (back,), (vmem,))
    landed = communicate(
        send_back_z,
        3,
        array(ROWS, PLANES, 128),
        (ROWS, ROWS, 1),
        (rows.reshape(8, 4, PLANES, 128),),
    )
    rotated = compute(restore, array(PLANES, ROWS, 128), [], (landed.reshape(ROWS * PLANES, 128),), (vmem,))
    return rotated.reshape(PLANES, 1, ROWS * 128), projections.reshape(2, 32, 128)


def solution(mesh):
    return jax.shard_map(
        local,
        mesh=mesh,
        in_specs=(P("gz", "gy", None), P(), P(), P("gy"), P("gy"), P("gy"), P("gy"), P()),
        out_specs=(P("gz", "gy", None), P("gz", "gy", None)),
        check_vma=False,
    )
```

```python
import functools

import jax
import jax.numpy as jnp
from jax import lax
from jax.experimental import pallas as pl
from jax.experimental.pallas import tpu as pltpu
from jax.sharding import PartitionSpec as P

TAPS = 64
ROWS = 32
PLANES = 40
DEPTH = 160
PLACES = 16
TILTS = 8
SLOPE = 4
F32 = jnp.float32
BF16 = jnp.bfloat16
VMEM_BYTES = 48 * 1024 * 1024


def tap_weight(offset, fraction):
    moved = offset.astype(F32) - fraction
    inside = (offset >= 1 - TAPS // 2) & (offset <= TAPS // 2)
    angle = jnp.pi * moved
    centre = moved == 0.0
    ratio = jnp.sin(angle) / jnp.where(centre, 1.0, angle)
    sinc = jnp.where(centre, 1.0, ratio)
    value = sinc * (0.5 + 0.5 * jnp.cos(jnp.pi * moved / (TAPS // 2 + 1)))
    return jnp.where(inside, value, 0.0)


def halves(value):
    high = value.astype(BF16)
    return high, (value - high.astype(F32)).astype(BF16)


def product(left, right):
    left_high, left_low = left
    right_high, right_low = right
    dot = functools.partial(jnp.dot, preferred_element_type=F32)
    return dot(left_high, right_high) + (dot(left_low, right_high) + dot(left_high, right_low))


def iota(shape, axis):
    return lax.broadcasted_iota(jnp.int32, shape, axis)


def band(row, rows, start=0, step=1):
    wide = jnp.broadcast_to(row, (rows, row.shape[1]))
    return pltpu.roll(wide, start, 1, stride=step, stride_axis=0)


def block(ref, index):
    return ref.at[pl.ds(pl.multiple_of(PLANES * index, 8), PLANES)]


def loop(start, stop, act):
    def body(d, carry):
        act(d)
        return carry

    lax.fori_loop(start, stop, body, 0)


def shear_x(offs, fracs, planes, arrive, out, taps):
    first = lax.axis_index("gz") * PLANES
    sub = iota((8, 128), 0)
    for part in range(PLANES // 8):
        off = jnp.zeros((8, 128), jnp.int32)
        frac = jnp.zeros((8, 128), F32)
        for s in range(8):
            off = jnp.where(sub == s, offs[first + 8 * part + s], off)
            frac = jnp.where(sub == s, fracs[first + 8 * part + s], frac)
        for side in range(2):
            lane = iota((8, 128), 1) + 128 * side
            weights = tap_weight(128 - lane - off, frac)
            taps[8 * part : 8 * part + 8, 128 * side : 128 * side + 128] = weights
        taps[8 * part : 8 * part + 8, 256:384] = jnp.zeros((8, 128), F32)
    row = iota((ROWS, 128), 0)

    def plane(z, carry):
        matrix = band(taps[pl.ds(z, 1), :], 128)
        total = product(halves(planes[z]), halves(matrix))
        after = jnp.where(row < ROWS - 1, pltpu.roll(total[:, :128], ROWS - 1, 0), 0.0)
        before = jnp.where(row > 0, pltpu.roll(total[:, 256:], 1, 0), 0.0)
        out[pl.ds(z, ROWS, stride=PLANES), :] = total[:, 128:256] + (after + before)
        return carry

    arrive()
    lax.fori_loop(0, PLANES, plane, 0, unroll=4)


def shear_z(h, lines, params, out, taps, mixed):
    lane = iota((8, 256), 1)
    target = jnp.where(lane < DEPTH, lane, lane - 256)
    off = params[:, 2, :][:, 0:1].astype(jnp.int32)
    frac = params[:, 3, :][:, 0:1]
    taps[0:4, :] = tap_weight(target[0:4] - off, frac)
    for n in range(4):
        source = halves(lines[640 * h + DEPTH * n : 640 * h + DEPTH * n + DEPTH, :])
        for odd in range(2):
            matrix = band(taps[n : n + 1, :], DEPTH // 2, odd, 2)[:, :DEPTH]
            value = product(halves(matrix), source)
            mixed[pl.ds(2 * n + odd, DEPTH // 2, stride=8), :] = value
    for part in range(5):
        turned = mixed[128 * part : 128 * part + 128, :].T
        for p in range(PLACES):
            row = 640 * h + PLANES * p + 8 * part
            out[row : row + 8, :] = turned[8 * p : 8 * p + 8, :]


def exchange(values):
    lane = iota((8, 128), 1)
    values = list(values)
    for step in (1, 2, 4, 8, 16):
        shift = 1 if step == 1 else 4 * step
        keep = (lane // shift) % 2 == 0
        for low in range(32):
            if low & step == 0:
                a, b = values[low], values[low | step]
                values[low] = jnp.where(keep, a, pltpu.roll(b, shift, 1))
                values[low | step] = jnp.where(keep, pltpu.roll(a, 128 - shift, 1), b)
    return values


def tile(ref, index):
    return ref.at[pl.ds(pl.multiple_of(8 * index, 8), 8)]


def shear_y(blocks, params, out, taps, before, after):
    def unpack(part):
        values = exchange([tile(blocks, 5 * i + part)[...] for i in range(32)])
        for i in range(32):
            tile(before, 32 * part + i)[...] = values[i]

    loop(0, 5, unpack)
    start = 8 * (lax.axis_index("gy") // 8 % 4)
    pick = iota((8, 128), 1) == start + iota((8, 128), 0)
    off = jnp.sum(jnp.where(pick, params[0:1, :], 0.0), axis=1, keepdims=True)
    frac = jnp.sum(jnp.where(pick, params[1:2, :], 0.0), axis=1, keepdims=True)
    lane = iota((8, 256), 1)
    target = jnp.where(lane < 128, lane, lane - 256)
    taps[...] = tap_weight(-target - off.astype(jnp.int32), frac)

    for x in range(8):
        matrix = band(taps[x : x + 1, :], 128)[:, :128]
        value = product(halves(before[pl.ds(x, DEPTH, stride=8), :]), halves(matrix))
        after[pl.ds(x, DEPTH, stride=8), :] = value

    def pack(part):
        values = exchange([tile(after, 32 * part + i)[...] for i in range(32)])
        for i in range(32):
            tile(out, 5 * i + part)[...] = values[i]

    loop(0, 5, pack)


def project(slopes, after, projections, table):
    lane = iota((8, 128), 1)
    zero = jnp.zeros((8, 128), F32)
    count = 2 * SLOPE + 1
    sums, totals = [zero] * count, [zero] * count
    for z in range(DEPTH):
        value = after[8 * z : 8 * z + 8, :]
        for i in range(count):
            lift = (i - SLOPE) * (2 * z - DEPTH) * 128 // (16 * DEPTH)
            following = (i - SLOPE) * (2 * z + 2 - DEPTH) * 128 // (16 * DEPTH)
            sums[i] = sums[i] + value
            if z == DEPTH - 1 or lift != following:
                moved = sums[i]
                if lift > 0:
                    moved = jnp.where(lane < 128 - lift, pltpu.roll(moved, 128 - lift, 1), 0.0)
                elif lift < 0:
                    moved = jnp.where(lane >= -lift, pltpu.roll(moved, -lift, 1), 0.0)
                totals[i] = totals[i] + moved
                sums[i] = zero
    for i in range(count):
        table[i] = totals[i] * DEPTH ** (-0.5)
    for t in range(TILTS):
        projections[t] = table[slopes[t] + SLOPE]


def turn_back(h, blocks, out, turned):
    for part in range(5):
        tiles = [blocks[640 * h + 40 * p + 8 * part : 640 * h + 40 * p + 8 * part + 8, :] for p in range(PLACES)]
        turned[128 * part : 128 * part + 128, :] = jnp.concatenate(tiles, axis=0).T
    for n in range(4):
        for odd in range(2):
            value = turned[pl.ds(2 * n + odd, DEPTH // 2, stride=8), :]
            out[pl.ds(640 * h + DEPTH * n + odd, DEPTH // 2, stride=2), :] = value


def restore(lines, out):
    for z in range(PLANES):
        out[z] = lines[pl.ds(z, ROWS, stride=PLANES), :]


def copy_to(src, dst, send, recv, g, j):
    return pltpu.make_async_remote_copy(
        src_ref=src,
        dst_ref=dst,
        send_sem=send,
        recv_sem=recv,
        device_id={"gz": g, "gy": j},
        device_id_type=pl.DeviceIdType.MESH,
    )


def signal(g, j):
    pl.semaphore_signal(
        pltpu.get_barrier_semaphore(),
        inc=1,
        device_id={"gz": g, "gy": j},
        device_id_type=pl.DeviceIdType.MESH,
    )


def rotate(
    x_offs, x_fracs, z_off, z_frac, slopes, y_offs, y_fracs, volume,
    landed, projections,
    planes, lines, gathered, mixed, outgoing, columns, before, after, returning, returned, rows,
    params, z_params, y_params, x_taps, z_taps, y_taps, table, terms,
    load, local, z_send, z_recv, xy_send, xy_recv, back_send, back_recv, home_send, home_recv,
    p_send, p_recv, t_send, t_recv,
):
    g, j = lax.axis_index("gz"), lax.axis_index("gy")
    p, n, core = j // 8, (j // 2) % 4, j % 2
    w = 4 * g + n

    def at_z(t):
        return t // 4, 8 * p + 2 * (t % 4) + core

    def at_xy(t, c):
        return g, 8 * t + 2 * n + c

    row = 16 * core + w
    home_j = 4 * row + p // 4
    owner_g = (j // 4) % 16 // 4

    def owner_j(b):
        return 8 * (4 * (j % 4) + b) + 2 * ((j // 4) % 4) + j // 64

    def is_self(a, b):
        return jnp.logical_and(a == g, b == j)

    loads = [
        pltpu.make_async_copy(volume.at[pl.ds(8 * i, 8)], planes.at[pl.ds(8 * i, 8)], load.at[i]) for i in range(5)
    ]
    for item in loads:
        item.start()
    loop(1, PLACES, lambda d: signal(*at_z((w + d) % PLACES)))
    for c in range(2):
        loop(1, PLACES, lambda d: signal(*at_xy((p + d) % PLACES, c)))
    signal(*at_xy(p, 1 - core))
    mine = is_self(owner_g, owner_j(g))
    for b in range(4):
        pl.when(jnp.logical_not(is_self(owner_g, owner_j(b))))(lambda b=b: signal(owner_g, owner_j(b)))
    own_home = is_self(p % 4, home_j)
    pl.when(jnp.logical_not(own_home))(lambda: signal(p % 4, home_j))

    params[...] = jnp.zeros((8, 128), F32)
    params[0:1, 0:32] = y_offs[...].astype(F32)
    params[1:2, 0:32] = y_fracs[...]
    params[2:3, :] = jnp.full((1, 128), z_off[0], jnp.int32).astype(F32)
    params[3:4, :] = jnp.full((1, 128), z_frac[0], F32)

    def arrive():
        for item in loads:
            item.wait()

    shear_x(x_offs, x_fracs, planes, arrive, lines, x_taps)
    greeted = 15 + 31 + 5 - (home_j == j).astype(jnp.int32) - mine.astype(jnp.int32)
    pl.semaphore_wait(pltpu.get_barrier_semaphore(), greeted)

    def z_param(d):
        t = 4 * g + (n + d) % 4
        return copy_to(params, z_params.at[n], p_send.at[d], p_recv.at[n], *at_z(t))

    def z_param_in(d):
        s = (n + 4 - d) % 4
        return copy_to(params, z_params.at[s], p_send.at[d], p_recv.at[s], *at_z(4 * g + s))

    y_out = copy_to(params, y_params, p_send.at[4], p_recv.at[4], owner_g, owner_j(g))
    y_in = copy_to(params, y_params, p_send.at[4], p_recv.at[4], p % 4, home_j)
    y_own = pltpu.make_async_copy(params, y_params, local.at[0])
    z_own = pltpu.make_async_copy(params, z_params.at[n], local.at[1])
    loop(1, 4, lambda d: z_param(d).start())
    pl.when(jnp.logical_not(mine))(lambda: y_out.start())
    pl.when(mine)(lambda: y_own.start())
    z_own.start()

    def z_out(h, d):
        t = (w + d) % PLACES
        dst = block(gathered, 16 * h + 4 * n + g)
        return copy_to(block(lines, 16 * h + t), dst, z_send.at[h, d], z_recv.at[h, w], *at_z(t))

    def z_in(h, d):
        s = (w + PLACES - d) % PLACES
        dst = block(gathered, 16 * h + 4 * (s % 4) + s // 4)
        return copy_to(block(lines, 16 * h + s), dst, z_send.at[h, d], z_recv.at[h, s], *at_z(s))

    z_owns = [
        pltpu.make_async_copy(block(lines, 16 * h + w), block(gathered, 16 * h + 4 * n + g), local.at[2 + h])
        for h in range(2)
    ]
    for h in range(2):
        loop(1, PLACES, lambda d: z_out(h, d).start())
        z_owns[h].start()
    z_own.wait()
    loop(1, 4, lambda d: z_param_in(d).wait_recv())

    def xy_out(h, d):
        t = (p + d) % PLACES
        dst = block(columns, 2 * p + core)
        return copy_to(block(outgoing, 16 * h + t), dst, xy_send.at[h, d], xy_recv.at[2 * p + core], *at_xy(t, h))

    def xy_in(c, d):
        s = (p + PLACES - d) % PLACES
        src = block(outgoing, 16 * core + s)
        return copy_to(src, block(columns, 2 * s + c), xy_send.at[0, d], xy_recv.at[2 * s + c], *at_xy(s, c))

    xy_own = pltpu.make_async_copy(block(outgoing, 16 * core + p), block(columns, 2 * p + core), local.at[4])

    def middle(h):
        z_owns[h].wait()
        loop(1, PLACES, lambda d: z_in(h, d).wait_recv())
        shear_z(h, gathered, z_params, outgoing, z_taps, mixed)
        loop(1, PLACES, lambda d: xy_out(h, d).start())
        pl.when(core != h)(lambda: xy_out(h, 0).start())
        pl.when(core == h)(lambda: xy_own.start())

    def back_out(c, d):
        t = (p + d) % PLACES
        dst = block(returned, 16 * core + p)
        return copy_to(block(returning, 2 * t + c), dst, back_send.at[c, d], back_recv.at[core, p], *at_xy(t, c))

    def back_in(h, d):
        s = (p + PLACES - d) % PLACES
        src = block(returning, 2 * s + core)
        return copy_to(src, block(returned, 16 * h + s), back_send.at[0, d], back_recv.at[h, s], *at_xy(s, h))

    back_own = pltpu.make_async_copy(block(returning, 2 * p + core), block(returned, 16 * core + p), local.at[5])

    def columns_here():
        for c in range(2):
            loop(1, PLACES, lambda d: xy_in(c, d).wait_recv())
        xy_in(1 - core, 0).wait_recv()
        xy_own.wait()
        shear_y(columns, y_params, returning, y_taps, before, after)
        for c in range(2):
            loop(1, PLACES, lambda d: back_out(c, d).start())
        back_out(1 - core, 0).start()
        back_own.start()

    def home_out(h, d):
        t = (w + d) % PLACES
        src = block(rows, 16 * h + 4 * (t % 4) + t // 4)
        return copy_to(src, block(landed, 16 * h + w), home_send.at[h, d], home_recv.at[h, w], *at_z(t))

    def home_in(h, d):
        s = (w + PLACES - d) % PLACES
        src = block(rows, 16 * h + 4 * (s % 4) + s // 4)
        return copy_to(src, block(landed, 16 * h + s), home_send.at[h, d], home_recv.at[h, s], *at_z(s))

    home_owns = [
        pltpu.make_async_copy(block(rows, 16 * h + 4 * n + g), block(landed, 16 * h + w), local.at[6 + h])
        for h in range(2)
    ]

    def finish(h):
        loop(1, PLACES, lambda d: back_in(h, d).wait_recv())
        pl.when(core != h)(lambda: back_in(h, 0).wait_recv())
        pl.when(core == h)(lambda: back_own.wait())
        turn_back(h, returned, rows, mixed)
        loop(1, PLACES, lambda d: home_out(h, d).start())
        home_owns[h].start()

    middle(0)
    pl.when(jnp.logical_not(own_home))(lambda: y_in.wait_recv())
    pl.when(mine)(lambda: y_own.wait())
    pl.when(core == 0)(columns_here)
    middle(1)
    finish(0)
    pl.when(core == 1)(columns_here)
    finish(1)

    project(slopes, after, terms, table)

    def term_out(b):
        return copy_to(
            terms.at[pl.ds(2 * b, 2)], projections.at[:, p % 4], t_send.at[b], t_recv.at[p % 4], b, home_j
        )

    def term_in(b):
        return copy_to(
            terms.at[pl.ds(2 * b, 2)], projections.at[:, b], t_send.at[b], t_recv.at[b], owner_g, owner_j(b)
        )

    def term_own():
        return pltpu.make_async_copy(terms.at[pl.ds(2 * g, 2)], projections.at[:, p % 4], local.at[0])

    for b in range(4):
        pl.when(jnp.logical_not(is_self(b, home_j)))(lambda b=b: term_out(b).start())
    pl.when(home_j == j)(lambda: term_own().start())

    loop(1, 4, lambda d: z_param(d).wait_send())
    pl.when(jnp.logical_not(mine))(lambda: y_out.wait_send())
    for h in range(2):
        loop(1, PLACES, lambda d: z_out(h, d).wait_send())
        loop(1, PLACES, lambda d: xy_out(h, d).wait_send())
        pl.when(core != h)(lambda h=h: xy_out(h, 0).wait_send())
        loop(1, PLACES, lambda d: back_out(h, d).wait_send())
    back_out(1 - core, 0).wait_send()
    pl.when(home_j == j)(lambda: term_own().wait())
    for b in range(4):
        pl.when(jnp.logical_not(is_self(b, home_j)))(lambda b=b: term_out(b).wait_send())
        pl.when(jnp.logical_not(is_self(owner_g, owner_j(b))))(lambda b=b: term_in(b).wait_recv())
    for h in range(2):
        loop(1, PLACES, lambda d: home_out(h, d).wait_send())
        home_owns[h].wait()
        loop(1, PLACES, lambda d: home_in(h, d).wait_recv())


def local(volume, x_offsets, x_fracs, z_offsets, z_fracs, y_offsets, y_fracs, slopes):
    array = lambda *shape: jax.ShapeDtypeStruct(shape, F32)
    vmem = lambda *shape: pltpu.VMEM(shape, F32)
    many = lambda *shape: pltpu.SemaphoreType.DMA(shape)
    smem = pltpu.SMEM
    whole = ROWS * PLANES
    spaces = (smem, smem, smem, smem, smem, pltpu.VMEM, pltpu.VMEM, pl.ANY)
    landed, projections = pl.pallas_call(
        rotate,
        out_shape=(array(whole, 128), array(2, 4, 8, 128)),
        in_specs=[pl.BlockSpec(memory_space=space) for space in spaces],
        out_specs=[pl.BlockSpec(memory_space=pl.ANY)] * 2,
        scratch_shapes=[
            vmem(PLANES, ROWS, 128),
            vmem(whole, 128),
            vmem(whole, 128),
            vmem(whole // 2, 128),
            *[vmem(whole, 128)] * 7,
            vmem(8, 128),
            vmem(4, 8, 128),
            vmem(8, 128),
            vmem(PLANES, 384),
            vmem(8, 256),
            vmem(8, 256),
            vmem(2 * SLOPE + 1, 8, 128),
            vmem(TILTS, 8, 128),
            many(5),
            many(8),
            many(2, PLACES),
            many(2, PLACES),
            many(2, PLACES),
            many(2 * PLACES),
            many(2, PLACES),
            many(2, PLACES),
            many(2, PLACES),
            many(2, PLACES),
            many(5),
            many(5),
            many(4),
            many(4),
        ],
        compiler_params=pltpu.CompilerParams(
            vmem_limit_bytes=VMEM_BYTES, collective_id=0, has_side_effects=True
        ),
    )(
        x_offsets,
        x_fracs,
        z_offsets,
        z_fracs,
        slopes,
        y_offsets.reshape(1, 32),
        y_fracs.reshape(1, 32),
        volume.reshape(PLANES, ROWS, 128),
    )
    rotated = pl.pallas_call(
        restore,
        out_shape=array(PLANES, ROWS, 128),
        in_specs=[pl.BlockSpec(memory_space=pltpu.VMEM)],
        compiler_params=pltpu.CompilerParams(vmem_limit_bytes=VMEM_BYTES),
    )(landed)
    return rotated.reshape(PLANES, 1, ROWS * 128), projections.reshape(2, 32, 128)


def solution(mesh):
    return jax.shard_map(
        local,
        mesh=mesh,
        in_specs=(P("gz", "gy", None), P(), P(), P("gy"), P("gy"), P("gy"), P("gy"), P()),
        out_specs=(P("gz", "gy", None), P("gz", "gy", None)),
        check_vma=False,
    )
```

```python
import functools

import jax
import jax.numpy as jnp
from jax import lax
from jax.experimental import pallas as pl
from jax.experimental.pallas import tpu as pltpu
from jax.sharding import PartitionSpec as P

TAPS = 64
ROWS = 32
PLANES = 40
DEPTH = 160
PLACES = 16
PARTS = ((0, 3), (3, 5))
TILTS = 8
SLOPE = 4
F32 = jnp.float32
BF16 = jnp.bfloat16
VMEM_BYTES = 48 * 1024 * 1024
ALL_VMEM_BYTES = 67043328


def tap_weight(offset, fraction):
    moved = offset.astype(F32) - fraction
    inside = (offset >= 1 - TAPS // 2) & (offset <= TAPS // 2)
    angle = jnp.pi * moved
    centre = moved == 0.0
    ratio = jnp.sin(angle) / jnp.where(centre, 1.0, angle)
    sinc = jnp.where(centre, 1.0, ratio)
    value = sinc * (0.5 + 0.5 * jnp.cos(jnp.pi * moved / (TAPS // 2 + 1)))
    return jnp.where(inside, value, 0.0)


def halves(value):
    high = value.astype(BF16)
    return high, (value - high.astype(F32)).astype(BF16)


def product(left, right):
    left_high, left_low = left
    right_high, right_low = right
    dot = functools.partial(jnp.dot, preferred_element_type=F32)
    return dot(left_high, right_high) + (dot(left_low, right_high) + dot(left_high, right_low))


def iota(shape, axis):
    return lax.broadcasted_iota(jnp.int32, shape, axis)


def band(row, rows, start=0, step=1):
    wide = jnp.broadcast_to(row, (rows, row.shape[1]))
    return pltpu.roll(wide, start, 1, stride=step, stride_axis=0)


def block(ref, index):
    return ref.at[pl.ds(pl.multiple_of(PLANES * index, 8), PLANES)]


def part_of(ref, index, k):
    first, last = PARTS[k]
    return ref.at[pl.ds(pl.multiple_of(PLANES * index + 8 * first, 8), 8 * (last - first))]


def loop(start, stop, act):
    def body(d, carry):
        act(d)
        return carry

    lax.fori_loop(start, stop, body, 0)


def shear_x(offs, fracs, planes, arrive, out, taps):
    first = lax.axis_index("gz") * PLANES
    sub = iota((8, 128), 0)
    for part in range(PLANES // 8):
        off = jnp.zeros((8, 128), jnp.int32)
        frac = jnp.zeros((8, 128), F32)
        for s in range(8):
            off = jnp.where(sub == s, offs[first + 8 * part + s], off)
            frac = jnp.where(sub == s, fracs[first + 8 * part + s], frac)
        for side in range(2):
            lane = iota((8, 128), 1) + 128 * side
            weights = tap_weight(128 - lane - off, frac)
            taps[8 * part : 8 * part + 8, 128 * side : 128 * side + 128] = weights
        taps[8 * part : 8 * part + 8, 256:384] = jnp.zeros((8, 128), F32)
    row = iota((ROWS, 128), 0)

    def plane(z, carry):
        matrix = band(taps[pl.ds(z, 1), :], 128)
        total = product(halves(planes[z]), halves(matrix))
        after = jnp.where(row < ROWS - 1, pltpu.roll(total[:, :128], ROWS - 1, 0), 0.0)
        before = jnp.where(row > 0, pltpu.roll(total[:, 256:], 1, 0), 0.0)
        out[pl.ds(z, ROWS, stride=PLANES), :] = total[:, 128:256] + (after + before)
        return carry

    arrive()
    lax.fori_loop(0, PLANES, plane, 0, unroll=4)


def prepare_z(params, highs, lows, taps):
    lane = iota((8, 256), 1)
    target = jnp.where(lane < DEPTH, lane, lane - 256)
    off = params[:, 2, :][:, 0:1].astype(jnp.int32)
    frac = params[:, 3, :][:, 0:1]
    taps[0:4, :] = tap_weight(target[0:4] - off, frac)
    for n in range(4):
        for odd in range(2):
            matrix = band(taps[n : n + 1, :], DEPTH // 2, odd, 2)[:, :DEPTH]
            highs[2 * n + odd], lows[2 * n + odd] = halves(matrix)


def shear_z(h, lines, highs, lows, out, mixed):
    for n in range(4):
        source = halves(lines[640 * h + DEPTH * n : 640 * h + DEPTH * n + DEPTH, :])
        for odd in range(2):
            value = product((highs[2 * n + odd], lows[2 * n + odd]), source)
            mixed[pl.ds(2 * n + odd, DEPTH // 2, stride=8), :] = value
    for part in range(5):
        turned = mixed[128 * part : 128 * part + 128, :].T
        for p in range(PLACES):
            row = 640 * h + PLANES * p + 8 * part
            out[row : row + 8, :] = turned[8 * p : 8 * p + 8, :]


def exchange(values):
    lane = iota((8, 128), 1)
    values = list(values)
    for step in (1, 2, 4, 8, 16):
        shift = 1 if step == 1 else 4 * step
        keep = (lane // shift) % 2 == 0
        for low in range(32):
            if low & step == 0:
                a, b = values[low], values[low | step]
                values[low] = jnp.where(keep, a, pltpu.roll(b, shift, 1))
                values[low | step] = jnp.where(keep, pltpu.roll(a, 128 - shift, 1), b)
    return values


def tile(ref, index):
    return ref.at[pl.ds(pl.multiple_of(8 * index, 8), 8)]


def prepare_y(params, highs, lows, taps):
    start = 8 * (lax.axis_index("gy") // 8 % 4)
    pick = iota((8, 128), 1) == start + iota((8, 128), 0)
    off = jnp.sum(jnp.where(pick, params[0:1, :], 0.0), axis=1, keepdims=True)
    frac = jnp.sum(jnp.where(pick, params[1:2, :], 0.0), axis=1, keepdims=True)
    lane = iota((8, 256), 1)
    target = jnp.where(lane < 128, lane, lane - 256)
    taps[...] = tap_weight(-target - off.astype(jnp.int32), frac)
    for x in range(8):
        highs[x], lows[x] = halves(band(taps[x : x + 1, :], 128)[:, :128])


def shear_y(k, blocks, highs, lows, out, before, after):
    first, last = PARTS[k]

    def unpack(part):
        values = exchange([tile(blocks, 5 * i + part)[...] for i in range(32)])
        for i in range(32):
            tile(before, 32 * part + i)[...] = values[i]

    loop(first, last, unpack)
    for x in range(8):
        rows = pl.ds(256 * first + x, 32 * (last - first), stride=8)
        after[rows, :] = product(halves(before[rows, :]), (highs[x], lows[x]))

    def pack(part):
        values = exchange([tile(after, 32 * part + i)[...] for i in range(32)])
        for i in range(32):
            tile(out, 5 * i + part)[...] = values[i]

    loop(first, last, pack)


def project(slopes, after, projections, table):
    lane = iota((8, 128), 1)
    zero = jnp.zeros((8, 128), F32)
    count = 2 * SLOPE + 1
    sums, totals = [zero] * count, [zero] * count
    for z in range(DEPTH):
        value = after[8 * z : 8 * z + 8, :]
        for i in range(count):
            lift = (i - SLOPE) * (2 * z - DEPTH) * 128 // (16 * DEPTH)
            following = (i - SLOPE) * (2 * z + 2 - DEPTH) * 128 // (16 * DEPTH)
            sums[i] = sums[i] + value
            if z == DEPTH - 1 or lift != following:
                moved = sums[i]
                if lift > 0:
                    moved = jnp.where(lane < 128 - lift, pltpu.roll(moved, 128 - lift, 1), 0.0)
                elif lift < 0:
                    moved = jnp.where(lane >= -lift, pltpu.roll(moved, -lift, 1), 0.0)
                totals[i] = totals[i] + moved
                sums[i] = zero
    for i in range(count):
        table[i] = totals[i] * DEPTH ** (-0.5)
    for t in range(TILTS):
        projections[t] = table[slopes[t] + SLOPE]


def turn_back(h, k, blocks, out, turned):
    first, last = PARTS[k]
    for part in range(first, last):
        tiles = [blocks[640 * h + 40 * p + 8 * part : 640 * h + 40 * p + 8 * part + 8, :] for p in range(PLACES)]
        turned[128 * part : 128 * part + 128, :] = jnp.concatenate(tiles, axis=0).T
    count = 16 * (last - first)
    for n in range(4):
        for odd in range(2):
            value = turned[pl.ds(128 * first + 2 * n + odd, count, stride=8), :]
            out[pl.ds(640 * h + DEPTH * n + 32 * first + odd, count, stride=2), :] = value


def restore(lines, terms, out, projections):
    for z in range(8):
        for part in range(ROWS // 8):
            out[z, 8 * part : 8 * part + 8, :] = lines[8 * part : 8 * part + 8, z, :]
    projections[...] = terms[...]


def copy_to(src, dst, send, recv, g, j):
    return pltpu.make_async_remote_copy(
        src_ref=src,
        dst_ref=dst,
        send_sem=send,
        recv_sem=recv,
        device_id={"gz": g, "gy": j},
        device_id_type=pl.DeviceIdType.MESH,
    )


def signal(g, j):
    pl.semaphore_signal(
        pltpu.get_barrier_semaphore(),
        inc=1,
        device_id={"gz": g, "gy": j},
        device_id_type=pl.DeviceIdType.MESH,
    )


def rotate(
    x_offs_in, x_fracs_in, z_off_in, z_frac_in, slopes_in, y_offs_in, y_fracs_in, volume,
    landed, projections,
    planes, lines, gathered, mixed, outgoing, columns, before, after, returning, returned, rows,
    x_offs, x_fracs, z_off, z_frac, slopes, y_offs, y_fracs,
    z_highs, z_lows, y_highs, y_lows,
    params, z_params, y_params, x_taps, z_taps, y_taps, table, terms,
    load, local, back_local, z_send, z_recv, xy_send, xy_recv, back_send, back_recv, home_send, home_recv,
    p_send, p_recv, t_send, t_recv,
):
    g, j = lax.axis_index("gz"), lax.axis_index("gy")
    p, n, core = j // 8, (j // 2) % 4, j % 2
    w = 4 * g + n

    def at_z(t):
        return t // 4, 8 * p + 2 * (t % 4) + core

    def at_xy(t, c):
        return g, 8 * t + 2 * n + c

    row = 16 * core + w
    home_j = 4 * row + p // 4
    owner_g = (j // 4) % 16 // 4

    def owner_j(b):
        return 8 * (4 * (j % 4) + b) + 2 * ((j // 4) % 4) + j // 64

    def is_self(a, b):
        return jnp.logical_and(a == g, b == j)

    loads = [
        pltpu.make_async_copy(volume.at[pl.ds(8 * i, 8)], planes.at[pl.ds(8 * i, 8)], load.at[i]) for i in range(5)
    ]
    smalls = (
        (x_offs_in, x_offs),
        (x_fracs_in, x_fracs),
        (y_offs_in, y_offs),
        (y_fracs_in, y_fracs),
        (z_off_in, z_off),
        (z_frac_in, z_frac),
        (slopes_in, slopes),
    )
    smalls = [pltpu.make_async_copy(src, dst, load.at[5 + i]) for i, (src, dst) in enumerate(smalls)]
    for item in smalls + loads:
        item.start()
    loop(1, PLACES, lambda d: signal(*at_z((w + d) % PLACES)))
    for c in range(2):
        loop(1, PLACES, lambda d: signal(*at_xy((p + d) % PLACES, c)))
    signal(*at_xy(p, 1 - core))
    mine = is_self(owner_g, owner_j(g))
    for b in range(4):
        pl.when(jnp.logical_not(is_self(owner_g, owner_j(b))))(lambda b=b: signal(owner_g, owner_j(b)))
    own_home = is_self(p % 4, home_j)
    pl.when(jnp.logical_not(own_home))(lambda: signal(p % 4, home_j))

    for item in smalls:
        item.wait()
    params[...] = jnp.zeros((8, 128), F32)
    params[0:1, 0:32] = y_offs[...].astype(F32)
    params[1:2, 0:32] = y_fracs[...]
    params[2:3, :] = jnp.full((1, 128), z_off[0], jnp.int32).astype(F32)
    params[3:4, :] = jnp.full((1, 128), z_frac[0], F32)

    def arrive():
        for item in loads:
            item.wait()

    shear_x(x_offs, x_fracs, planes, arrive, lines, x_taps)
    greeted = 15 + 31 + 5 - (home_j == j).astype(jnp.int32) - mine.astype(jnp.int32)
    pl.semaphore_wait(pltpu.get_barrier_semaphore(), greeted)

    def z_param(d):
        t = 4 * g + (n + d) % 4
        return copy_to(params, z_params.at[n], p_send.at[d], p_recv.at[n], *at_z(t))

    def z_param_in(d):
        s = (n + 4 - d) % 4
        return copy_to(params, z_params.at[s], p_send.at[d], p_recv.at[s], *at_z(4 * g + s))

    y_out = copy_to(params, y_params, p_send.at[4], p_recv.at[4], owner_g, owner_j(g))
    y_in = copy_to(params, y_params, p_send.at[4], p_recv.at[4], p % 4, home_j)
    y_own = pltpu.make_async_copy(params, y_params, local.at[0])
    z_own = pltpu.make_async_copy(params, z_params.at[n], local.at[1])
    loop(1, 4, lambda d: z_param(d).start())
    pl.when(jnp.logical_not(mine))(lambda: y_out.start())
    pl.when(mine)(lambda: y_own.start())
    z_own.start()

    def z_out(h, d):
        t = (w + d) % PLACES
        dst = block(gathered, 16 * h + 4 * n + g)
        return copy_to(block(lines, 16 * h + t), dst, z_send.at[h, d], z_recv.at[h, w], *at_z(t))

    def z_in(h, d):
        s = (w + PLACES - d) % PLACES
        dst = block(gathered, 16 * h + 4 * (s % 4) + s // 4)
        return copy_to(block(lines, 16 * h + s), dst, z_send.at[h, d], z_recv.at[h, s], *at_z(s))

    z_owns = [
        pltpu.make_async_copy(block(lines, 16 * h + w), block(gathered, 16 * h + 4 * n + g), local.at[2 + h])
        for h in range(2)
    ]
    for h in range(2):
        loop(1, PLACES, lambda d: z_out(h, d).start())
        z_owns[h].start()
    z_own.wait()
    loop(1, 4, lambda d: z_param_in(d).wait_recv())
    prepare_z(z_params, z_highs, z_lows, z_taps)
    pl.when(jnp.logical_not(own_home))(lambda: y_in.wait_recv())
    pl.when(mine)(lambda: y_own.wait())
    prepare_y(y_params, y_highs, y_lows, y_taps)

    def xy_out(k, h, d):
        t = (p + d) % PLACES
        dst = part_of(columns, 2 * p + core, k)
        src = part_of(outgoing, 16 * h + t, k)
        return copy_to(src, dst, xy_send.at[k, h, d], xy_recv.at[k, 2 * p + core], *at_xy(t, h))

    def xy_in(k, c, d):
        s = (p + PLACES - d) % PLACES
        src = part_of(outgoing, 16 * core + s, k)
        dst = part_of(columns, 2 * s + c, k)
        return copy_to(src, dst, xy_send.at[k, 0, d], xy_recv.at[k, 2 * s + c], *at_xy(s, c))

    xy_own = pltpu.make_async_copy(block(outgoing, 16 * core + p), block(columns, 2 * p + core), local.at[4])

    def middle(h):
        z_owns[h].wait()
        loop(1, PLACES, lambda d: z_in(h, d).wait_recv())
        shear_z(h, gathered, z_highs, z_lows, outgoing, mixed)
        for k in range(2):
            loop(1, PLACES, lambda d: xy_out(k, h, d).start())
            pl.when(core != h)(lambda: xy_out(k, h, 0).start())
        pl.when(core == h)(lambda: xy_own.start())

    def back_out(k, c, d):
        t = (p + d) % PLACES
        src = part_of(returning, 2 * t + c, k)
        dst = part_of(returned, 16 * core + p, k)
        return copy_to(src, dst, back_send.at[k, c, d], back_recv.at[k, core, p], *at_xy(t, c))

    def back_in(k, h, d):
        s = (p + PLACES - d) % PLACES
        src = part_of(returning, 2 * s + core, k)
        dst = part_of(returned, 16 * h + s, k)
        return copy_to(src, dst, back_send.at[k, 0, d], back_recv.at[k, h, s], *at_xy(s, h))

    back_owns = [
        pltpu.make_async_copy(
            part_of(returning, 2 * p + core, k), part_of(returned, 16 * core + p, k), back_local.at[k]
        )
        for k in range(2)
    ]

    def columns_here():
        xy_own.wait()
        for k in range(2):
            for c in range(2):
                loop(1, PLACES, lambda d: xy_in(k, c, d).wait_recv())
            xy_in(k, 1 - core, 0).wait_recv()
            shear_y(k, columns, y_highs, y_lows, returning, before, after)
            for c in range(2):
                loop(1, PLACES, lambda d: back_out(k, c, d).start())
            back_out(k, 1 - core, 0).start()
            back_owns[k].start()

    def home_out(h, t):
        src = block(rows, 16 * h + 4 * (t % 4) + t // 4)
        return copy_to(src, block(landed, 16 * h + w), home_send.at[h, t], home_recv.at[h, w], *at_z(t))

    def home_in(h, d):
        s = (w + PLACES - d) % PLACES
        src = block(rows, 16 * h + 4 * (s % 4) + s // 4)
        return copy_to(src, block(landed, 16 * h + s), home_send.at[h, s], home_recv.at[h, s], *at_z(s))

    home_owns = [
        pltpu.make_async_copy(block(rows, 16 * h + 4 * n + g), block(landed, 16 * h + w), local.at[6 + h])
        for h in range(2)
    ]

    def finish(h):
        for k in range(2):
            loop(1, PLACES, lambda d: back_in(k, h, d).wait_recv())
            pl.when(core != h)(lambda: back_in(k, h, 0).wait_recv())
            pl.when(core == h)(lambda: back_owns[k].wait())
            turn_back(h, k, returned, rows, mixed)

            def send(d):
                t = 8 * k + (w + d) % 8
                pl.when(t != w)(lambda: home_out(h, t).start())

            loop(0, 8, send)
        home_owns[h].start()

    middle(0)
    pl.when(core == 0)(columns_here)
    middle(1)
    finish(0)
    pl.when(core == 1)(columns_here)
    finish(1)

    project(slopes, after, terms, table)

    def term_out(b):
        return copy_to(
            terms.at[pl.ds(2 * b, 2)], projections.at[:, p % 4], t_send.at[b], t_recv.at[p % 4], b, home_j
        )

    def term_in(b):
        return copy_to(
            terms.at[pl.ds(2 * b, 2)], projections.at[:, b], t_send.at[b], t_recv.at[b], owner_g, owner_j(b)
        )

    def term_own():
        return pltpu.make_async_copy(terms.at[pl.ds(2 * g, 2)], projections.at[:, p % 4], local.at[0])

    for b in range(4):
        pl.when(jnp.logical_not(is_self(b, home_j)))(lambda b=b: term_out(b).start())
    pl.when(home_j == j)(lambda: term_own().start())

    loop(1, 4, lambda d: z_param(d).wait_send())
    pl.when(jnp.logical_not(mine))(lambda: y_out.wait_send())
    for h in range(2):
        loop(1, PLACES, lambda d: z_out(h, d).wait_send())
        for k in range(2):
            loop(1, PLACES, lambda d: xy_out(k, h, d).wait_send())
            pl.when(core != h)(lambda h=h, k=k: xy_out(k, h, 0).wait_send())
            loop(1, PLACES, lambda d: back_out(k, h, d).wait_send())
    for k in range(2):
        back_out(k, 1 - core, 0).wait_send()
    pl.when(home_j == j)(lambda: term_own().wait())
    for b in range(4):
        pl.when(jnp.logical_not(is_self(b, home_j)))(lambda b=b: term_out(b).wait_send())
        pl.when(jnp.logical_not(is_self(owner_g, owner_j(b))))(lambda b=b: term_in(b).wait_recv())
    for h in range(2):
        loop(1, PLACES, lambda d: home_out(h, (w + d) % PLACES).wait_send())
        home_owns[h].wait()
        loop(1, PLACES, lambda d: home_in(h, d).wait_recv())


def local(volume, x_offsets, x_fracs, z_offsets, z_fracs, y_offsets, y_fracs, slopes):
    array = lambda *shape: jax.ShapeDtypeStruct(shape, F32)
    vmem = lambda *shape: pltpu.VMEM(shape, F32)
    many = lambda *shape: pltpu.SemaphoreType.DMA(shape)
    smem = pltpu.SMEM
    whole = ROWS * PLANES
    landed, projections = pl.pallas_call(
        rotate,
        out_shape=(array(whole, 128), array(2, 4, 8, 128)),
        in_specs=[pl.BlockSpec(memory_space=pltpu.HBM)] * 8,
        out_specs=[pl.BlockSpec(memory_space=pl.ANY)] * 2,
        scratch_shapes=[
            vmem(PLANES, ROWS, 128),
            vmem(whole, 128),
            vmem(whole, 128),
            vmem(whole // 2, 128),
            *[vmem(whole, 128)] * 7,
            smem((DEPTH,), jnp.int32),
            smem((DEPTH,), F32),
            smem((1,), jnp.int32),
            smem((1,), F32),
            smem((TILTS,), jnp.int32),
            pltpu.VMEM((1, 32), jnp.int32),
            vmem(1, 32),
            *[pltpu.VMEM((8, DEPTH // 2, DEPTH), BF16)] * 2,
            *[pltpu.VMEM((8, 128, 128), BF16)] * 2,
            vmem(8, 128),
            vmem(4, 8, 128),
            vmem(8, 128),
            vmem(PLANES, 384),
            vmem(8, 256),
            vmem(8, 256),
            vmem(2 * SLOPE + 1, 8, 128),
            vmem(TILTS, 8, 128),
            many(12),
            many(8),
            many(2),
            many(2, PLACES),
            many(2, PLACES),
            many(2, 2, PLACES),
            many(2, 2 * PLACES),
            many(2, 2, PLACES),
            many(2, 2, PLACES),
            many(2, PLACES),
            many(2, PLACES),
            many(5),
            many(5),
            many(4),
            many(4),
        ],
        compiler_params=pltpu.CompilerParams(
            vmem_limit_bytes=ALL_VMEM_BYTES, collective_id=0, has_side_effects=True
        ),
    )(
        x_offsets,
        x_fracs,
        z_offsets,
        z_fracs,
        slopes,
        y_offsets.reshape(1, 32),
        y_fracs.reshape(1, 32),
        volume.reshape(PLANES, ROWS, 128),
    )
    rotated, projections = pl.pallas_call(
        restore,
        grid=(PLANES // 8,),
        out_shape=(array(PLANES, ROWS, 128), array(2, 4, 8, 128)),
        in_specs=[
            pl.BlockSpec((ROWS, 8, 128), lambda i: (0, i, 0)),
            pl.BlockSpec((2, 4, 8, 128), lambda i: (0, 0, 0, 0)),
        ],
        out_specs=[
            pl.BlockSpec((8, ROWS, 128), lambda i: (i, 0, 0)),
            pl.BlockSpec((2, 4, 8, 128), lambda i: (0, 0, 0, 0)),
        ],
        compiler_params=pltpu.CompilerParams(vmem_limit_bytes=ALL_VMEM_BYTES),
    )(landed.reshape(ROWS, PLANES, 128), projections)
    return rotated.reshape(PLANES, 1, ROWS * 128), projections.reshape(2, 32, 128)


def solution(mesh):
    return jax.shard_map(
        local,
        mesh=mesh,
        in_specs=(P("gz", "gy", None), P(), P(), P("gy"), P("gy"), P("gy"), P("gy"), P()),
        out_specs=(P("gz", "gy", None), P("gz", "gy", None)),
        check_vma=False,
    )
```

```python
import functools

import jax
import jax.numpy as jnp
from jax import lax
from jax.experimental import pallas as pl
from jax.experimental.pallas import tpu as pltpu
from jax.sharding import PartitionSpec as P

TAPS = 64
ROWS = 32
PLANES = 40
DEPTH = 160
PLACES = 16
PARTS = ((0, 3), (3, 5))
TILTS = 8
SLOPE = 4
F32 = jnp.float32
BF16 = jnp.bfloat16
VMEM_BYTES = 48 * 1024 * 1024
ALL_VMEM_BYTES = 67043328


def tap_weight(offset, fraction):
    moved = offset.astype(F32) - fraction
    inside = (offset >= 1 - TAPS // 2) & (offset <= TAPS // 2)
    angle = jnp.pi * moved
    centre = moved == 0.0
    ratio = jnp.sin(angle) / jnp.where(centre, 1.0, angle)
    sinc = jnp.where(centre, 1.0, ratio)
    value = sinc * (0.5 + 0.5 * jnp.cos(jnp.pi * moved / (TAPS // 2 + 1)))
    return jnp.where(inside, value, 0.0)


def halves(value):
    high = value.astype(BF16)
    return high, (value - high.astype(F32)).astype(BF16)


def product(left, right):
    left_high, left_low = left
    right_high, right_low = right
    dot = functools.partial(jnp.dot, preferred_element_type=F32)
    return dot(left_high, right_high) + (dot(left_low, right_high) + dot(left_high, right_low))


def iota(shape, axis):
    return lax.broadcasted_iota(jnp.int32, shape, axis)


def band(row, rows, start=0, step=1):
    wide = jnp.broadcast_to(row, (rows, row.shape[1]))
    return pltpu.roll(wide, start, 1, stride=step, stride_axis=0)


def block(ref, index):
    return ref.at[pl.ds(pl.multiple_of(PLANES * index, 8), PLANES)]


def far_first(i):
    return 8 + (i + 1) // 2 * (1 - 2 * (i % 2))


def part_of(ref, index, k):
    first, last = PARTS[k]
    return ref.at[pl.ds(pl.multiple_of(PLANES * index + 8 * first, 8), 8 * (last - first))]


def loop(start, stop, act):
    def body(d, carry):
        act(d)
        return carry

    lax.fori_loop(start, stop, body, 0)


def shear_x(offs, fracs, planes, arrive, out, taps):
    first = lax.axis_index("gz") * PLANES
    sub = iota((8, 128), 0)
    for part in range(PLANES // 8):
        off = jnp.zeros((8, 128), jnp.int32)
        frac = jnp.zeros((8, 128), F32)
        for s in range(8):
            off = jnp.where(sub == s, offs[first + 8 * part + s], off)
            frac = jnp.where(sub == s, fracs[first + 8 * part + s], frac)
        for side in range(2):
            lane = iota((8, 128), 1) + 128 * side
            weights = tap_weight(128 - lane - off, frac)
            taps[8 * part : 8 * part + 8, 128 * side : 128 * side + 128] = weights
        taps[8 * part : 8 * part + 8, 256:384] = jnp.zeros((8, 128), F32)
    row = iota((ROWS, 128), 0)

    def plane(z, carry):
        matrix_high, matrix_low = halves(band(taps[pl.ds(z, 1), :], 128))
        high, low = halves(planes[z])
        both = jnp.dot(jnp.concatenate([high, low], axis=0), matrix_high, preferred_element_type=F32)
        total = both[:ROWS] + (both[ROWS:] + jnp.dot(high, matrix_low, preferred_element_type=F32))
        after = jnp.where(row < ROWS - 1, pltpu.roll(total[:, :128], ROWS - 1, 0), 0.0)
        before = jnp.where(row > 0, pltpu.roll(total[:, 256:], 1, 0), 0.0)
        out[pl.ds(z, ROWS, stride=PLANES), :] = total[:, 128:256] + (after + before)
        return carry

    arrive()
    lax.fori_loop(0, PLANES, plane, 0, unroll=4)


def prepare_z(params, highs, lows, taps):
    lane = iota((8, 256), 1)
    target = jnp.where(lane < DEPTH, lane, lane - 256)
    off = params[:, 2, :][:, 0:1].astype(jnp.int32)
    frac = params[:, 3, :][:, 0:1]
    taps[0:4, :] = tap_weight(target[0:4] - off, frac)
    for n in range(4):
        for odd in range(2):
            matrix = band(taps[n : n + 1, :], DEPTH // 2, odd, 2)[:, :DEPTH]
            highs[2 * n + odd], lows[2 * n + odd] = halves(matrix)


def shear_z(h, lines, highs, lows, out, mixed):
    for n in range(4):
        source = halves(lines[640 * h + DEPTH * n : 640 * h + DEPTH * n + DEPTH, :])
        for odd in range(2):
            value = product((highs[2 * n + odd], lows[2 * n + odd]), source)
            mixed[pl.ds(2 * n + odd, DEPTH // 2, stride=8), :] = value
    for part in range(5):
        turned = mixed[128 * part : 128 * part + 128, :].T
        for p in range(PLACES):
            row = 640 * h + PLANES * p + 8 * part
            out[row : row + 8, :] = turned[8 * p : 8 * p + 8, :]


def exchange(values):
    lane = iota((8, 128), 1)
    values = list(values)
    for step in (1, 2, 4, 8, 16):
        shift = 1 if step == 1 else 4 * step
        keep = (lane // shift) % 2 == 0
        for low in range(32):
            if low & step == 0:
                a, b = values[low], values[low | step]
                values[low] = jnp.where(keep, a, pltpu.roll(b, shift, 1))
                values[low | step] = jnp.where(keep, pltpu.roll(a, 128 - shift, 1), b)
    return values


def tile(ref, index):
    return ref.at[pl.ds(pl.multiple_of(8 * index, 8), 8)]


def prepare_y(params, highs, lows, taps):
    start = 8 * (lax.axis_index("gy") // 8 % 4)
    pick = iota((8, 128), 1) == start + iota((8, 128), 0)
    off = jnp.sum(jnp.where(pick, params[0:1, :], 0.0), axis=1, keepdims=True)
    frac = jnp.sum(jnp.where(pick, params[1:2, :], 0.0), axis=1, keepdims=True)
    lane = iota((8, 256), 1)
    target = jnp.where(lane < 128, lane, lane - 256)
    taps[...] = tap_weight(-target - off.astype(jnp.int32), frac)
    for x in range(8):
        highs[x], lows[x] = halves(band(taps[x : x + 1, :], 128)[:, :128])


def shear_y(k, blocks, highs, lows, out, before, after):
    first, last = PARTS[k]

    def unpack(part):
        values = exchange([tile(blocks, 5 * i + part)[...] for i in range(32)])
        for i in range(32):
            tile(before, 32 * part + i)[...] = values[i]

    loop(first, last, unpack)
    for x in range(8):
        rows = pl.ds(256 * first + x, 32 * (last - first), stride=8)
        after[rows, :] = product(halves(before[rows, :]), (highs[x], lows[x]))

    def pack(part):
        values = exchange([tile(after, 32 * part + i)[...] for i in range(32)])
        for i in range(32):
            tile(out, 5 * i + part)[...] = values[i]

    loop(first, last, pack)


def project(slopes, after, projections, table):
    lane = iota((8, 128), 1)
    zero = jnp.zeros((8, 128), F32)
    count = 2 * SLOPE + 1
    sums, totals = [zero] * count, [zero] * count
    for z in range(DEPTH):
        value = after[8 * z : 8 * z + 8, :]
        for i in range(count):
            lift = (i - SLOPE) * (2 * z - DEPTH) * 128 // (16 * DEPTH)
            following = (i - SLOPE) * (2 * z + 2 - DEPTH) * 128 // (16 * DEPTH)
            sums[i] = sums[i] + value
            if z == DEPTH - 1 or lift != following:
                moved = sums[i]
                if lift > 0:
                    moved = jnp.where(lane < 128 - lift, pltpu.roll(moved, 128 - lift, 1), 0.0)
                elif lift < 0:
                    moved = jnp.where(lane >= -lift, pltpu.roll(moved, -lift, 1), 0.0)
                totals[i] = totals[i] + moved
                sums[i] = zero
    for i in range(count):
        table[i] = totals[i] * DEPTH ** (-0.5)
    for t in range(TILTS):
        projections[t] = table[slopes[t] + SLOPE]


def turn_back(h, k, blocks, out, turned):
    first, last = PARTS[k]
    for part in range(first, last):
        tiles = [blocks[640 * h + 40 * p + 8 * part : 640 * h + 40 * p + 8 * part + 8, :] for p in range(PLACES)]
        turned[128 * part : 128 * part + 128, :] = jnp.concatenate(tiles, axis=0).T
    count = 16 * (last - first)
    for n in range(4):
        for odd in range(2):
            value = turned[pl.ds(128 * first + 2 * n + odd, count, stride=8), :]
            out[pl.ds(640 * h + DEPTH * n + 32 * first + odd, count, stride=2), :] = value


def restore(lines, terms, out, projections):
    for z in range(PLANES):
        out[z] = lines[pl.ds(z, ROWS, stride=PLANES), :]
    projections[...] = terms[...]


def copy_to(src, dst, send, recv, g, j):
    return pltpu.make_async_remote_copy(
        src_ref=src,
        dst_ref=dst,
        send_sem=send,
        recv_sem=recv,
        device_id={"gz": g, "gy": j},
        device_id_type=pl.DeviceIdType.MESH,
    )


def signal(g, j):
    pl.semaphore_signal(
        pltpu.get_barrier_semaphore(),
        inc=1,
        device_id={"gz": g, "gy": j},
        device_id_type=pl.DeviceIdType.MESH,
    )


def rotate(
    x_offs_in, x_fracs_in, z_off_in, z_frac_in, slopes_in, y_offs_in, y_fracs_in, volume,
    landed, projections,
    planes, lines, gathered, mixed, outgoing, columns, before, after, returning, returned, rows,
    x_offs, x_fracs, z_off, z_frac, slopes, y_offs, y_fracs,
    z_highs, z_lows, y_highs, y_lows,
    params, z_params, y_params, x_taps, z_taps, y_taps, table, terms,
    load, local, back_local, z_send, z_recv, xy_send, xy_recv, back_send, back_recv, home_send, home_recv,
    p_send, p_recv, t_send, t_recv,
):
    g, j = lax.axis_index("gz"), lax.axis_index("gy")
    p, n, core = j // 8, (j // 2) % 4, j % 2
    w = 4 * g + n

    def at_z(t):
        return t // 4, 8 * p + 2 * (t % 4) + core

    def at_xy(t, c):
        return g, 8 * t + 2 * n + c

    row = 16 * core + w
    home_j = 4 * row + p // 4
    owner_g = (j // 4) % 16 // 4

    def owner_j(b):
        return 8 * (4 * (j % 4) + b) + 2 * ((j // 4) % 4) + j // 64

    def is_self(a, b):
        return jnp.logical_and(a == g, b == j)

    loads = [
        pltpu.make_async_copy(volume.at[pl.ds(8 * i, 8)], planes.at[pl.ds(8 * i, 8)], load.at[i]) for i in range(5)
    ]
    smalls = (
        (x_offs_in, x_offs),
        (x_fracs_in, x_fracs),
        (y_offs_in, y_offs),
        (y_fracs_in, y_fracs),
        (z_off_in, z_off),
        (z_frac_in, z_frac),
        (slopes_in, slopes),
    )
    smalls = [pltpu.make_async_copy(src, dst, load.at[5 + i]) for i, (src, dst) in enumerate(smalls)]
    for item in smalls + loads:
        item.start()
    loop(1, PLACES, lambda d: signal(*at_z((w + d) % PLACES)))
    for c in range(2):
        loop(1, PLACES, lambda d: signal(*at_xy((p + d) % PLACES, c)))
    signal(*at_xy(p, 1 - core))
    mine = is_self(owner_g, owner_j(g))
    for b in range(4):
        pl.when(jnp.logical_not(is_self(owner_g, owner_j(b))))(lambda b=b: signal(owner_g, owner_j(b)))
    own_home = is_self(p % 4, home_j)
    pl.when(jnp.logical_not(own_home))(lambda: signal(p % 4, home_j))

    for item in smalls:
        item.wait()
    params[...] = jnp.zeros((8, 128), F32)
    params[0:1, 0:32] = y_offs[...].astype(F32)
    params[1:2, 0:32] = y_fracs[...]
    params[2:3, :] = jnp.full((1, 128), z_off[0], jnp.int32).astype(F32)
    params[3:4, :] = jnp.full((1, 128), z_frac[0], F32)

    def arrive():
        for item in loads:
            item.wait()

    shear_x(x_offs, x_fracs, planes, arrive, lines, x_taps)
    greeted = 15 + 31 + 5 - (home_j == j).astype(jnp.int32) - mine.astype(jnp.int32)
    pl.semaphore_wait(pltpu.get_barrier_semaphore(), greeted)

    def z_param(d):
        t = 4 * g + (n + d) % 4
        return copy_to(params, z_params.at[n], p_send.at[d], p_recv.at[n], *at_z(t))

    def z_param_in(d):
        s = (n + 4 - d) % 4
        return copy_to(params, z_params.at[s], p_send.at[d], p_recv.at[s], *at_z(4 * g + s))

    y_out = copy_to(params, y_params, p_send.at[4], p_recv.at[4], owner_g, owner_j(g))
    y_in = copy_to(params, y_params, p_send.at[4], p_recv.at[4], p % 4, home_j)
    y_own = pltpu.make_async_copy(params, y_params, local.at[0])
    z_own = pltpu.make_async_copy(params, z_params.at[n], local.at[1])
    loop(1, 4, lambda d: z_param(d).start())
    pl.when(jnp.logical_not(mine))(lambda: y_out.start())
    pl.when(mine)(lambda: y_own.start())
    z_own.start()

    def z_out(h, d):
        t = (w + d) % PLACES
        dst = block(gathered, 16 * h + 4 * n + g)
        return copy_to(block(lines, 16 * h + t), dst, z_send.at[h, d], z_recv.at[h, w], *at_z(t))

    def z_in(h, d):
        s = (w + PLACES - d) % PLACES
        dst = block(gathered, 16 * h + 4 * (s % 4) + s // 4)
        return copy_to(block(lines, 16 * h + s), dst, z_send.at[h, d], z_recv.at[h, s], *at_z(s))

    z_owns = [
        pltpu.make_async_copy(block(lines, 16 * h + w), block(gathered, 16 * h + 4 * n + g), local.at[2 + h])
        for h in range(2)
    ]
    for h in range(2):
        loop(0, PLACES - 1, lambda i: z_out(h, far_first(i)).start())
    for h in range(2):
        z_owns[h].start()
    z_own.wait()
    loop(1, 4, lambda d: z_param_in(d).wait_recv())
    prepare_z(z_params, z_highs, z_lows, z_taps)
    pl.when(jnp.logical_not(own_home))(lambda: y_in.wait_recv())
    pl.when(mine)(lambda: y_own.wait())
    prepare_y(y_params, y_highs, y_lows, y_taps)

    def xy_out(k, h, d):
        t = (p + d) % PLACES
        dst = part_of(columns, 2 * p + core, k)
        src = part_of(outgoing, 16 * h + t, k)
        return copy_to(src, dst, xy_send.at[k, h, d], xy_recv.at[k, 2 * p + core], *at_xy(t, h))

    def xy_in(k, c, d):
        s = (p + PLACES - d) % PLACES
        src = part_of(outgoing, 16 * core + s, k)
        dst = part_of(columns, 2 * s + c, k)
        return copy_to(src, dst, xy_send.at[k, 0, d], xy_recv.at[k, 2 * s + c], *at_xy(s, c))

    xy_own = pltpu.make_async_copy(block(outgoing, 16 * core + p), block(columns, 2 * p + core), local.at[4])

    def middle(h):
        z_owns[h].wait()
        loop(1, PLACES, lambda d: z_in(h, d).wait_recv())
        shear_z(h, gathered, z_highs, z_lows, outgoing, mixed)
        for k in range(2):
            loop(1, PLACES, lambda d: xy_out(k, h, d).start())
            pl.when(core != h)(lambda: xy_out(k, h, 0).start())
        pl.when(core == h)(lambda: xy_own.start())

    def back_out(k, c, d):
        t = (p + d) % PLACES
        src = part_of(returning, 2 * t + c, k)
        dst = part_of(returned, 16 * core + p, k)
        return copy_to(src, dst, back_send.at[k, c, d], back_recv.at[k, core, p], *at_xy(t, c))

    def back_in(k, h, d):
        s = (p + PLACES - d) % PLACES
        src = part_of(returning, 2 * s + core, k)
        dst = part_of(returned, 16 * h + s, k)
        return copy_to(src, dst, back_send.at[k, 0, d], back_recv.at[k, h, s], *at_xy(s, h))

    back_owns = [
        pltpu.make_async_copy(
            part_of(returning, 2 * p + core, k), part_of(returned, 16 * core + p, k), back_local.at[k]
        )
        for k in range(2)
    ]

    def columns_here():
        xy_own.wait()
        for k in range(2):
            for c in range(2):
                loop(1, PLACES, lambda d: xy_in(k, c, d).wait_recv())
            xy_in(k, 1 - core, 0).wait_recv()
            shear_y(k, columns, y_highs, y_lows, returning, before, after)
            for c in range(2):
                loop(1, PLACES, lambda d: back_out(k, c, d).start())
            back_out(k, 1 - core, 0).start()
            back_owns[k].start()

    def home_out(h, t):
        src = block(rows, 16 * h + 4 * (t % 4) + t // 4)
        return copy_to(src, block(landed, 16 * h + w), home_send.at[h, t], home_recv.at[h, w], *at_z(t))

    def home_in(h, d):
        s = (w + PLACES - d) % PLACES
        src = block(rows, 16 * h + 4 * (s % 4) + s // 4)
        return copy_to(src, block(landed, 16 * h + s), home_send.at[h, s], home_recv.at[h, s], *at_z(s))

    home_owns = [
        pltpu.make_async_copy(block(rows, 16 * h + 4 * n + g), block(landed, 16 * h + w), local.at[6 + h])
        for h in range(2)
    ]

    def finish(h):
        for k in range(2):
            loop(1, PLACES, lambda d: back_in(k, h, d).wait_recv())
            pl.when(core != h)(lambda: back_in(k, h, 0).wait_recv())
            pl.when(core == h)(lambda: back_owns[k].wait())
            turn_back(h, k, returned, rows, mixed)

            def send(i):
                t = (w + far_first(i)) % PLACES
                pl.when(t // 8 == k)(lambda: home_out(h, t).start())

            loop(0, PLACES - 1, send)
        home_owns[h].start()

    middle(0)
    pl.when(core == 0)(columns_here)
    middle(1)
    finish(0)
    pl.when(core == 1)(columns_here)
    finish(1)

    project(slopes, after, terms, table)

    def term_out(b):
        return copy_to(
            terms.at[pl.ds(2 * b, 2)], projections.at[:, p % 4], t_send.at[b], t_recv.at[p % 4], b, home_j
        )

    def term_in(b):
        return copy_to(
            terms.at[pl.ds(2 * b, 2)], projections.at[:, b], t_send.at[b], t_recv.at[b], owner_g, owner_j(b)
        )

    def term_own():
        return pltpu.make_async_copy(terms.at[pl.ds(2 * g, 2)], projections.at[:, p % 4], local.at[0])

    for b in range(4):
        pl.when(jnp.logical_not(is_self(b, home_j)))(lambda b=b: term_out(b).start())
    pl.when(home_j == j)(lambda: term_own().start())

    loop(1, 4, lambda d: z_param(d).wait_send())
    pl.when(jnp.logical_not(mine))(lambda: y_out.wait_send())
    for h in range(2):
        loop(1, PLACES, lambda d: z_out(h, d).wait_send())
        for k in range(2):
            loop(1, PLACES, lambda d: xy_out(k, h, d).wait_send())
            pl.when(core != h)(lambda h=h, k=k: xy_out(k, h, 0).wait_send())
            loop(1, PLACES, lambda d: back_out(k, h, d).wait_send())
    for k in range(2):
        back_out(k, 1 - core, 0).wait_send()
    pl.when(home_j == j)(lambda: term_own().wait())
    for b in range(4):
        pl.when(jnp.logical_not(is_self(b, home_j)))(lambda b=b: term_out(b).wait_send())
        pl.when(jnp.logical_not(is_self(owner_g, owner_j(b))))(lambda b=b: term_in(b).wait_recv())
    for h in range(2):
        loop(1, PLACES, lambda d: home_out(h, (w + d) % PLACES).wait_send())
        home_owns[h].wait()
        loop(1, PLACES, lambda d: home_in(h, d).wait_recv())


def local(volume, x_offsets, x_fracs, z_offsets, z_fracs, y_offsets, y_fracs, slopes):
    array = lambda *shape: jax.ShapeDtypeStruct(shape, F32)
    vmem = lambda *shape: pltpu.VMEM(shape, F32)
    many = lambda *shape: pltpu.SemaphoreType.DMA(shape)
    smem = pltpu.SMEM
    whole = ROWS * PLANES
    landed, projections = pl.pallas_call(
        rotate,
        out_shape=(array(whole, 128), array(2, 4, 8, 128)),
        in_specs=[pl.BlockSpec(memory_space=pltpu.HBM)] * 8,
        out_specs=[pl.BlockSpec(memory_space=pl.ANY)] * 2,
        scratch_shapes=[
            vmem(PLANES, ROWS, 128),
            vmem(whole, 128),
            vmem(whole, 128),
            vmem(whole // 2, 128),
            *[vmem(whole, 128)] * 7,
            smem((DEPTH,), jnp.int32),
            smem((DEPTH,), F32),
            smem((1,), jnp.int32),
            smem((1,), F32),
            smem((TILTS,), jnp.int32),
            pltpu.VMEM((1, 32), jnp.int32),
            vmem(1, 32),
            *[pltpu.VMEM((8, DEPTH // 2, DEPTH), BF16)] * 2,
            *[pltpu.VMEM((8, 128, 128), BF16)] * 2,
            vmem(8, 128),
            vmem(4, 8, 128),
            vmem(8, 128),
            vmem(PLANES, 384),
            vmem(8, 256),
            vmem(8, 256),
            vmem(2 * SLOPE + 1, 8, 128),
            vmem(TILTS, 8, 128),
            many(12),
            many(8),
            many(2),
            many(2, PLACES),
            many(2, PLACES),
            many(2, 2, PLACES),
            many(2, 2 * PLACES),
            many(2, 2, PLACES),
            many(2, 2, PLACES),
            many(2, PLACES),
            many(2, PLACES),
            many(5),
            many(5),
            many(4),
            many(4),
        ],
        compiler_params=pltpu.CompilerParams(
            vmem_limit_bytes=ALL_VMEM_BYTES, collective_id=0, has_side_effects=True
        ),
    )(
        x_offsets,
        x_fracs,
        z_offsets,
        z_fracs,
        slopes,
        y_offsets.reshape(1, 32),
        y_fracs.reshape(1, 32),
        volume.reshape(PLANES, ROWS, 128),
    )
    rotated, projections = pl.pallas_call(
        restore,
        out_shape=(array(PLANES, ROWS, 128), array(2, 4, 8, 128)),
        in_specs=[pl.BlockSpec(memory_space=pltpu.VMEM)] * 2,
        compiler_params=pltpu.CompilerParams(vmem_limit_bytes=VMEM_BYTES),
    )(landed, projections)
    return rotated.reshape(PLANES, 1, ROWS * 128), projections.reshape(2, 32, 128)


def solution(mesh):
    return jax.shard_map(
        local,
        mesh=mesh,
        in_specs=(P("gz", "gy", None), P(), P(), P("gy"), P("gy"), P("gy"), P("gy"), P()),
        out_specs=(P("gz", "gy", None), P("gz", "gy", None)),
        check_vma=False,
    )
```

```python
import functools

import jax
import jax.numpy as jnp
from jax import lax
from jax.experimental import pallas as pl
from jax.experimental.pallas import tpu as pltpu
from jax.sharding import PartitionSpec as P

TAPS = 64
ROWS = 32
PLANES = 40
DEPTH = 160
PLACES = 16
PARTS = ((0, 3), (3, 5))
TILTS = 8
SLOPE = 4
F32 = jnp.float32
BF16 = jnp.bfloat16
VMEM_BYTES = 48 * 1024 * 1024
ALL_VMEM_BYTES = 67043328


def tap_weight(offset, fraction):
    moved = offset.astype(F32) - fraction
    inside = (offset >= 1 - TAPS // 2) & (offset <= TAPS // 2)
    angle = jnp.pi * moved
    centre = moved == 0.0
    ratio = jnp.sin(angle) / jnp.where(centre, 1.0, angle)
    sinc = jnp.where(centre, 1.0, ratio)
    value = sinc * (0.5 + 0.5 * jnp.cos(jnp.pi * moved / (TAPS // 2 + 1)))
    return jnp.where(inside, value, 0.0)


def halves(value):
    high = value.astype(BF16)
    return high, (value - high.astype(F32)).astype(BF16)


def product(left, right):
    left_high, left_low = left
    right_high, right_low = right
    dot = functools.partial(jnp.dot, preferred_element_type=F32)
    return dot(left_high, right_high) + (dot(left_low, right_high) + dot(left_high, right_low))


def iota(shape, axis):
    return lax.broadcasted_iota(jnp.int32, shape, axis)


def band(row, rows, start=0, step=1):
    wide = jnp.broadcast_to(row, (rows, row.shape[1]))
    return pltpu.roll(wide, start, 1, stride=step, stride_axis=0)


def block(ref, index):
    return ref.at[pl.ds(pl.multiple_of(PLANES * index, 8), PLANES)]


def far_first(i):
    return 8 + (i + 1) // 2 * (1 - 2 * (i % 2))


PLANE_STEPS = (10, 6, 9, 11, 14, 2, 8, 5, 7, 13, 15, 4, 12, 1, 3)


def part_of(ref, index, k):
    first, last = PARTS[k]
    return ref.at[pl.ds(pl.multiple_of(PLANES * index + 8 * first, 8), 8 * (last - first))]


def loop(start, stop, act):
    def body(d, carry):
        act(d)
        return carry

    lax.fori_loop(start, stop, body, 0)


def shear_x(offs, fracs, planes, arrive, out, taps):
    first = lax.axis_index("gz") * PLANES
    sub = iota((8, 128), 0)
    for part in range(PLANES // 8):
        off = jnp.zeros((8, 128), jnp.int32)
        frac = jnp.zeros((8, 128), F32)
        for s in range(8):
            off = jnp.where(sub == s, offs[first + 8 * part + s], off)
            frac = jnp.where(sub == s, fracs[first + 8 * part + s], frac)
        for side in range(2):
            lane = iota((8, 128), 1) + 128 * side
            weights = tap_weight(128 - lane - off, frac)
            taps[8 * part : 8 * part + 8, 128 * side : 128 * side + 128] = weights
        taps[8 * part : 8 * part + 8, 256:384] = jnp.zeros((8, 128), F32)
    row = iota((ROWS, 128), 0)

    def plane(z, carry):
        matrix_high, matrix_low = halves(band(taps[pl.ds(z, 1), :], 128))
        high, low = halves(planes[z])
        both = jnp.dot(jnp.concatenate([high, low], axis=0), matrix_high, preferred_element_type=F32)
        total = both[:ROWS] + (both[ROWS:] + jnp.dot(high, matrix_low, preferred_element_type=F32))
        after = jnp.where(row < ROWS - 1, pltpu.roll(total[:, :128], ROWS - 1, 0), 0.0)
        before = jnp.where(row > 0, pltpu.roll(total[:, 256:], 1, 0), 0.0)
        out[pl.ds(z, ROWS, stride=PLANES), :] = total[:, 128:256] + (after + before)
        return carry

    arrive()
    lax.fori_loop(0, PLANES, plane, 0, unroll=10)


def prepare_z(params, highs, lows, taps):
    lane = iota((8, 256), 1)
    target = jnp.where(lane < DEPTH, lane, lane - 256)
    off = params[:, 2, :][:, 0:1].astype(jnp.int32)
    frac = params[:, 3, :][:, 0:1]
    taps[0:4, :] = tap_weight(target[0:4] - off, frac)
    for n in range(4):
        for odd in range(2):
            matrix = band(taps[n : n + 1, :], DEPTH // 2, odd, 2)[:, :DEPTH]
            highs[2 * n + odd], lows[2 * n + odd] = halves(matrix)


def shear_z(h, lines, highs, lows, out, mixed):
    for n in range(4):
        source = halves(lines[640 * h + DEPTH * n : 640 * h + DEPTH * n + DEPTH, :])
        for odd in range(2):
            value = product((highs[2 * n + odd], lows[2 * n + odd]), source)
            mixed[pl.ds(2 * n + odd, DEPTH // 2, stride=8), :] = value
    for part in range(5):
        turned = mixed[128 * part : 128 * part + 128, :].T
        for p in range(PLACES):
            row = 640 * h + PLANES * p + 8 * part
            out[row : row + 8, :] = turned[8 * p : 8 * p + 8, :]


def exchange(values):
    lane = iota((8, 128), 1)
    values = list(values)
    for step in (1, 2, 4, 8, 16):
        shift = 1 if step == 1 else 4 * step
        keep = (lane // shift) % 2 == 0
        for low in range(32):
            if low & step == 0:
                a, b = values[low], values[low | step]
                values[low] = jnp.where(keep, a, pltpu.roll(b, shift, 1))
                values[low | step] = jnp.where(keep, pltpu.roll(a, 128 - shift, 1), b)
    return values


def tile(ref, index):
    return ref.at[pl.ds(pl.multiple_of(8 * index, 8), 8)]


def prepare_y(params, highs, lows, taps):
    start = 8 * (lax.axis_index("gy") // 8 % 4)
    pick = iota((8, 128), 1) == start + iota((8, 128), 0)
    off = jnp.sum(jnp.where(pick, params[0:1, :], 0.0), axis=1, keepdims=True)
    frac = jnp.sum(jnp.where(pick, params[1:2, :], 0.0), axis=1, keepdims=True)
    lane = iota((8, 256), 1)
    target = jnp.where(lane < 128, lane, lane - 256)
    taps[...] = tap_weight(-target - off.astype(jnp.int32), frac)
    for x in range(8):
        highs[x], lows[x] = halves(band(taps[x : x + 1, :], 128)[:, :128])


def shear_y(k, blocks, highs, lows, out, before, after):
    first, last = PARTS[k]

    def unpack(part):
        values = exchange([tile(blocks, 5 * i + part)[...] for i in range(32)])
        for i in range(32):
            tile(before, 32 * part + i)[...] = values[i]

    loop(first, last, unpack)
    for x in range(8):
        rows = pl.ds(256 * first + x, 32 * (last - first), stride=8)
        after[rows, :] = product(halves(before[rows, :]), (highs[x], lows[x]))

    def pack(part):
        values = exchange([tile(after, 32 * part + i)[...] for i in range(32)])
        for i in range(32):
            tile(out, 5 * i + part)[...] = values[i]

    loop(first, last, pack)


def project(slopes, after, projections, table):
    lane = iota((8, 128), 1)
    zero = jnp.zeros((8, 128), F32)
    count = 2 * SLOPE + 1
    sums, totals = [zero] * count, [zero] * count
    for z in range(DEPTH):
        value = after[8 * z : 8 * z + 8, :]
        for i in range(count):
            lift = (i - SLOPE) * (2 * z - DEPTH) * 128 // (16 * DEPTH)
            following = (i - SLOPE) * (2 * z + 2 - DEPTH) * 128 // (16 * DEPTH)
            sums[i] = sums[i] + value
            if z == DEPTH - 1 or lift != following:
                moved = sums[i]
                if lift > 0:
                    moved = jnp.where(lane < 128 - lift, pltpu.roll(moved, 128 - lift, 1), 0.0)
                elif lift < 0:
                    moved = jnp.where(lane >= -lift, pltpu.roll(moved, -lift, 1), 0.0)
                totals[i] = totals[i] + moved
                sums[i] = zero
    for i in range(count):
        table[i] = totals[i] * DEPTH ** (-0.5)
    for t in range(TILTS):
        projections[t] = table[slopes[t] + SLOPE]


def turn_back(h, k, blocks, out, turned):
    first, last = PARTS[k]
    for part in range(first, last):
        tiles = [blocks[640 * h + 40 * p + 8 * part : 640 * h + 40 * p + 8 * part + 8, :] for p in range(PLACES)]
        turned[128 * part : 128 * part + 128, :] = jnp.concatenate(tiles, axis=0).T
    count = 16 * (last - first)
    for n in range(4):
        for odd in range(2):
            value = turned[pl.ds(128 * first + 2 * n + odd, count, stride=8), :]
            out[pl.ds(640 * h + DEPTH * n + 32 * first + odd, count, stride=2), :] = value


def restore(lines, terms, out, projections):
    for z in range(PLANES):
        out[z] = lines[pl.ds(z, ROWS, stride=PLANES), :]
    projections[...] = terms[...]


def copy_to(src, dst, send, recv, g, j):
    return pltpu.make_async_remote_copy(
        src_ref=src,
        dst_ref=dst,
        send_sem=send,
        recv_sem=recv,
        device_id={"gz": g, "gy": j},
        device_id_type=pl.DeviceIdType.MESH,
    )


def signal(g, j):
    pl.semaphore_signal(
        pltpu.get_barrier_semaphore(),
        inc=1,
        device_id={"gz": g, "gy": j},
        device_id_type=pl.DeviceIdType.MESH,
    )


def rotate(
    x_offs_in, x_fracs_in, z_off_in, z_frac_in, slopes_in, y_offs_in, y_fracs_in, volume,
    landed, projections,
    planes, lines, gathered, mixed, outgoing, columns, before, after, returning, returned, rows,
    x_offs, x_fracs, z_off, z_frac, slopes, y_offs, y_fracs,
    z_highs, z_lows, y_highs, y_lows,
    params, z_params, y_params, x_taps, z_taps, y_taps, table, terms,
    load, local, back_local, z_send, z_recv, xy_send, xy_recv, back_send, back_recv, home_send, home_recv,
    p_send, p_recv, t_send, t_recv,
):
    g, j = lax.axis_index("gz"), lax.axis_index("gy")
    p, n, core = j // 8, (j // 2) % 4, j % 2
    w = 4 * g + n

    def at_z(t):
        return t // 4, 8 * p + 2 * (t % 4) + core

    def at_xy(t, c):
        return g, 8 * t + 2 * n + c

    row = 16 * core + w
    home_j = 4 * row + p // 4
    owner_g = (j // 4) % 16 // 4

    def owner_j(b):
        return 8 * (4 * (j % 4) + b) + 2 * ((j // 4) % 4) + j // 64

    def is_self(a, b):
        return jnp.logical_and(a == g, b == j)

    loads = [
        pltpu.make_async_copy(volume.at[pl.ds(8 * i, 8)], planes.at[pl.ds(8 * i, 8)], load.at[i]) for i in range(5)
    ]
    smalls = (
        (x_offs_in, x_offs),
        (x_fracs_in, x_fracs),
        (y_offs_in, y_offs),
        (y_fracs_in, y_fracs),
        (z_off_in, z_off),
        (z_frac_in, z_frac),
        (slopes_in, slopes),
    )
    smalls = [pltpu.make_async_copy(src, dst, load.at[5 + i]) for i, (src, dst) in enumerate(smalls)]
    for item in smalls + loads:
        item.start()
    loop(1, PLACES, lambda d: signal(*at_z((w + d) % PLACES)))
    for c in range(2):
        loop(1, PLACES, lambda d: signal(*at_xy((p + d) % PLACES, c)))
    signal(*at_xy(p, 1 - core))
    mine = is_self(owner_g, owner_j(g))
    for b in range(4):
        pl.when(jnp.logical_not(is_self(owner_g, owner_j(b))))(lambda b=b: signal(owner_g, owner_j(b)))
    own_home = is_self(p % 4, home_j)
    pl.when(jnp.logical_not(own_home))(lambda: signal(p % 4, home_j))

    for item in smalls:
        item.wait()
    params[...] = jnp.zeros((8, 128), F32)
    params[0:1, 0:32] = y_offs[...].astype(F32)
    params[1:2, 0:32] = y_fracs[...]
    params[2:3, :] = jnp.full((1, 128), z_off[0], jnp.int32).astype(F32)
    params[3:4, :] = jnp.full((1, 128), z_frac[0], F32)

    def arrive():
        for item in loads:
            item.wait()

    shear_x(x_offs, x_fracs, planes, arrive, lines, x_taps)
    greeted = 15 + 31 + 5 - (home_j == j).astype(jnp.int32) - mine.astype(jnp.int32)
    pl.semaphore_wait(pltpu.get_barrier_semaphore(), greeted)

    def z_param(d):
        t = 4 * g + (n + d) % 4
        return copy_to(params, z_params.at[n], p_send.at[d], p_recv.at[n], *at_z(t))

    def z_param_in(d):
        s = (n + 4 - d) % 4
        return copy_to(params, z_params.at[s], p_send.at[d], p_recv.at[s], *at_z(4 * g + s))

    y_out = copy_to(params, y_params, p_send.at[4], p_recv.at[4], owner_g, owner_j(g))
    y_in = copy_to(params, y_params, p_send.at[4], p_recv.at[4], p % 4, home_j)
    y_own = pltpu.make_async_copy(params, y_params, local.at[0])
    z_own = pltpu.make_async_copy(params, z_params.at[n], local.at[1])
    loop(1, 4, lambda d: z_param(d).start())
    pl.when(jnp.logical_not(mine))(lambda: y_out.start())
    pl.when(mine)(lambda: y_own.start())
    z_own.start()

    def z_out(h, d):
        t = (w + d) % PLACES
        dst = block(gathered, 16 * h + 4 * n + g)
        return copy_to(block(lines, 16 * h + t), dst, z_send.at[h, d], z_recv.at[h, w], *at_z(t))

    def z_in(h, d):
        s = (w + PLACES - d) % PLACES
        dst = block(gathered, 16 * h + 4 * (s % 4) + s // 4)
        return copy_to(block(lines, 16 * h + s), dst, z_send.at[h, d], z_recv.at[h, s], *at_z(s))

    z_owns = [
        pltpu.make_async_copy(block(lines, 16 * h + w), block(gathered, 16 * h + 4 * n + g), local.at[2 + h])
        for h in range(2)
    ]
    for h in range(2):
        loop(0, PLACES - 1, lambda i: z_out(h, far_first(i)).start())
    for h in range(2):
        z_owns[h].start()
    z_own.wait()
    loop(1, 4, lambda d: z_param_in(d).wait_recv())
    prepare_z(z_params, z_highs, z_lows, z_taps)
    pl.when(jnp.logical_not(own_home))(lambda: y_in.wait_recv())
    pl.when(mine)(lambda: y_own.wait())
    prepare_y(y_params, y_highs, y_lows, y_taps)

    def xy_out(k, h, d):
        t = (p + d) % PLACES
        dst = part_of(columns, 2 * p + core, k)
        src = part_of(outgoing, 16 * h + t, k)
        return copy_to(src, dst, xy_send.at[k, h, d], xy_recv.at[k, 2 * p + core], *at_xy(t, h))

    def xy_in(k, c, d):
        s = (p + PLACES - d) % PLACES
        src = part_of(outgoing, 16 * core + s, k)
        dst = part_of(columns, 2 * s + c, k)
        return copy_to(src, dst, xy_send.at[k, 0, d], xy_recv.at[k, 2 * s + c], *at_xy(s, c))

    xy_own = pltpu.make_async_copy(block(outgoing, 16 * core + p), block(columns, 2 * p + core), local.at[4])

    def middle(h):
        z_owns[h].wait()
        loop(1, PLACES, lambda d: z_in(h, d).wait_recv())
        shear_z(h, gathered, z_highs, z_lows, outgoing, mixed)
        for k in range(2):
            for d in PLANE_STEPS:
                xy_out(k, h, d).start()
            pl.when(core != h)(lambda: xy_out(k, h, 0).start())
        pl.when(core == h)(lambda: xy_own.start())

    def back_out(k, c, d):
        t = (p + d) % PLACES
        src = part_of(returning, 2 * t + c, k)
        dst = part_of(returned, 16 * core + p, k)
        return copy_to(src, dst, back_send.at[k, c, d], back_recv.at[k, core, p], *at_xy(t, c))

    def back_in(k, h, d):
        s = (p + PLACES - d) % PLACES
        src = part_of(returning, 2 * s + core, k)
        dst = part_of(returned, 16 * h + s, k)
        return copy_to(src, dst, back_send.at[k, 0, d], back_recv.at[k, h, s], *at_xy(s, h))

    back_owns = [
        pltpu.make_async_copy(
            part_of(returning, 2 * p + core, k), part_of(returned, 16 * core + p, k), back_local.at[k]
        )
        for k in range(2)
    ]

    def columns_here():
        xy_own.wait()
        for k in range(2):
            for c in range(2):
                loop(1, PLACES, lambda d: xy_in(k, c, d).wait_recv())
            xy_in(k, 1 - core, 0).wait_recv()
            shear_y(k, columns, y_highs, y_lows, returning, before, after)
            for d in PLANE_STEPS:
                for c in range(2):
                    back_out(k, c, d).start()
            back_out(k, 1 - core, 0).start()
            back_owns[k].start()

    def home_out(h, t):
        src = block(rows, 16 * h + 4 * (t % 4) + t // 4)
        return copy_to(src, block(landed, 16 * h + w), home_send.at[h, t], home_recv.at[h, w], *at_z(t))

    def home_in(h, d):
        s = (w + PLACES - d) % PLACES
        src = block(rows, 16 * h + 4 * (s % 4) + s // 4)
        return copy_to(src, block(landed, 16 * h + s), home_send.at[h, s], home_recv.at[h, s], *at_z(s))

    home_owns = [
        pltpu.make_async_copy(block(rows, 16 * h + 4 * n + g), block(landed, 16 * h + w), local.at[6 + h])
        for h in range(2)
    ]

    def finish(h):
        for k in range(2):
            loop(1, PLACES, lambda d: back_in(k, h, d).wait_recv())
            pl.when(core != h)(lambda: back_in(k, h, 0).wait_recv())
            pl.when(core == h)(lambda: back_owns[k].wait())
            turn_back(h, k, returned, rows, mixed)

            def send(i):
                t = (w + far_first(i)) % PLACES
                pl.when(t // 8 == k)(lambda: home_out(h, t).start())

            loop(0, PLACES - 1, send)
        home_owns[h].start()

    middle(0)
    pl.when(core == 0)(columns_here)
    middle(1)
    finish(0)
    pl.when(core == 1)(columns_here)
    finish(1)

    project(slopes, after, terms, table)

    def term_out(b):
        return copy_to(
            terms.at[pl.ds(2 * b, 2)], projections.at[:, p % 4], t_send.at[b], t_recv.at[p % 4], b, home_j
        )

    def term_in(b):
        return copy_to(
            terms.at[pl.ds(2 * b, 2)], projections.at[:, b], t_send.at[b], t_recv.at[b], owner_g, owner_j(b)
        )

    def term_own():
        return pltpu.make_async_copy(terms.at[pl.ds(2 * g, 2)], projections.at[:, p % 4], local.at[0])

    for b in range(4):
        pl.when(jnp.logical_not(is_self(b, home_j)))(lambda b=b: term_out(b).start())
    pl.when(home_j == j)(lambda: term_own().start())

    loop(1, 4, lambda d: z_param(d).wait_send())
    pl.when(jnp.logical_not(mine))(lambda: y_out.wait_send())
    for h in range(2):
        loop(1, PLACES, lambda d: z_out(h, d).wait_send())
        for k in range(2):
            loop(1, PLACES, lambda d: xy_out(k, h, d).wait_send())
            pl.when(core != h)(lambda h=h, k=k: xy_out(k, h, 0).wait_send())
            loop(1, PLACES, lambda d: back_out(k, h, d).wait_send())
    for k in range(2):
        back_out(k, 1 - core, 0).wait_send()
    pl.when(home_j == j)(lambda: term_own().wait())
    for b in range(4):
        pl.when(jnp.logical_not(is_self(b, home_j)))(lambda b=b: term_out(b).wait_send())
        pl.when(jnp.logical_not(is_self(owner_g, owner_j(b))))(lambda b=b: term_in(b).wait_recv())
    for h in range(2):
        loop(1, PLACES, lambda d: home_out(h, (w + d) % PLACES).wait_send())
        home_owns[h].wait()
        loop(1, PLACES, lambda d: home_in(h, d).wait_recv())


def local(volume, x_offsets, x_fracs, z_offsets, z_fracs, y_offsets, y_fracs, slopes):
    array = lambda *shape: jax.ShapeDtypeStruct(shape, F32)
    vmem = lambda *shape: pltpu.VMEM(shape, F32)
    many = lambda *shape: pltpu.SemaphoreType.DMA(shape)
    smem = pltpu.SMEM
    whole = ROWS * PLANES
    landed, projections = pl.pallas_call(
        rotate,
        out_shape=(array(whole, 128), array(2, 4, 8, 128)),
        in_specs=[pl.BlockSpec(memory_space=pltpu.HBM)] * 8,
        out_specs=[pl.BlockSpec(memory_space=pl.ANY)] * 2,
        scratch_shapes=[
            vmem(PLANES, ROWS, 128),
            vmem(whole, 128),
            vmem(whole, 128),
            vmem(whole // 2, 128),
            *[vmem(whole, 128)] * 7,
            smem((DEPTH,), jnp.int32),
            smem((DEPTH,), F32),
            smem((1,), jnp.int32),
            smem((1,), F32),
            smem((TILTS,), jnp.int32),
            pltpu.VMEM((1, 32), jnp.int32),
            vmem(1, 32),
            *[pltpu.VMEM((8, DEPTH // 2, DEPTH), BF16)] * 2,
            *[pltpu.VMEM((8, 128, 128), BF16)] * 2,
            vmem(8, 128),
            vmem(4, 8, 128),
            vmem(8, 128),
            vmem(PLANES, 384),
            vmem(8, 256),
            vmem(8, 256),
            vmem(2 * SLOPE + 1, 8, 128),
            vmem(TILTS, 8, 128),
            many(12),
            many(8),
            many(2),
            many(2, PLACES),
            many(2, PLACES),
            many(2, 2, PLACES),
            many(2, 2 * PLACES),
            many(2, 2, PLACES),
            many(2, 2, PLACES),
            many(2, PLACES),
            many(2, PLACES),
            many(5),
            many(5),
            many(4),
            many(4),
        ],
        compiler_params=pltpu.CompilerParams(
            vmem_limit_bytes=ALL_VMEM_BYTES, collective_id=0, has_side_effects=True
        ),
    )(
        x_offsets,
        x_fracs,
        z_offsets,
        z_fracs,
        slopes,
        y_offsets.reshape(1, 32),
        y_fracs.reshape(1, 32),
        volume.reshape(PLANES, ROWS, 128),
    )
    rotated, projections = pl.pallas_call(
        restore,
        out_shape=(array(PLANES, ROWS, 128), array(2, 4, 8, 128)),
        in_specs=[pl.BlockSpec(memory_space=pltpu.VMEM)] * 2,
        compiler_params=pltpu.CompilerParams(vmem_limit_bytes=VMEM_BYTES),
    )(landed, projections)
    return rotated.reshape(PLANES, 1, ROWS * 128), projections.reshape(2, 32, 128)


def solution(mesh):
    return jax.shard_map(
        local,
        mesh=mesh,
        in_specs=(P("gz", "gy", None), P(), P(), P("gy"), P("gy"), P("gy"), P("gy"), P()),
        out_specs=(P("gz", "gy", None), P("gz", "gy", None)),
        check_vma=False,
    )
```
